32 devices in a mesh: lat: 8 (over y, x, core), ens: 4 (over z).
Axes of the slice: x: 2, y: 2, z: 4, core: 2. Of those that a mesh axis runs over, the one named last changes fastest.
Arguments:
- predicted_grid: bfloat16 [8, 36, 64, 1440], P('ens', None, 'lat'), may hold values from -6 to 6
- verifying_coefficients: float32 [36, 2, 16, 721], P(None, None, 'lat'), may hold values from -5 to 5
- weighted_polynomial_values: bfloat16 [16, 64, 721], P('lat'), may hold values from -0.75 to 0.75
- zonal_order_values: int32 [16], replicated, may hold values from 0 to 720, as said below
Outputs:
- prediction_sensitivity: bfloat16 [8, 36, 64, 1440], P('ens', None, 'lat')
- coefficient_error_mean: float32 [36, 2, 16], P(None, None, 'lat')
The draws below stay inside these ranges and needn't reach their ends.
Inputs may be any that keep to these rules, and one draw needn't show every extreme that they name: `zonal_order_values`: the wavenumbers are distinct, 0 and 720 are always among them; slot s belongs to index s // 2 of lat.
All inputs are finite; a program needn't handle non-finite values.
Results may differ from the reference program's by a relative error of at most 0.014.
Values may be sent and summed in bfloat16 or wider, within the bound.
A program may use at most 64 MiB of HBM per device.

```python
import math
import jax
import jax.numpy as jnp
from jax import lax

PREDICTED_VARS = 36
MERIDIAN_NODES = 1440
L = 720
DEGREE_RANGE = 721
REALIZATIONS = 8
PARALLEL_LINES = 64
ORDERS_KEPT = 16


def draw_zonal_order_values(key, part):
    first, second = jax.random.split(key)
    inner = 1 + jax.random.permutation(first, L - 1)[:ORDERS_KEPT - 2]
    chosen = jnp.concatenate([jnp.array([0, L], dtype=jnp.int32), inner.astype(jnp.int32)])
    return jax.random.permutation(second, chosen)


def levels(rng, extent, cuts, low, largest):
    def one(axis_at, shards_of):
        steps = jax.random.uniform(jax.random.fold_in(jax.random.fold_in(rng, 6), axis_at), (shards_of,), jnp.float32, low / len(cuts), largest / len(cuts))
        return jnp.repeat(jnp.exp(steps), extent[axis_at] // shards_of).reshape((-1,) + (1,) * (len(extent) - axis_at - 1))

    gain = one(*cuts[0])
    for cut in cuts[1:]:
        gain = gain * one(*cut)
    return gain


def scatter_about(stream_key, dims, deviation, limit, cuts=(), kind=jnp.bfloat16):
    entries = jax.random.normal(stream_key, dims, jnp.float32) * deviation
    if len(cuts) > 0:
        entries = levels(stream_key, dims, cuts, -0.22, 0.18) * entries
    return jnp.clip(entries, min=-limit, max=limit).astype(kind)


def setup_inputs(seed: int = 0) -> dict:
    key_of = jax.random.split(jax.random.key(seed), 5)
    return {
        "predicted_grid": scatter_about(key_of[0], (REALIZATIONS, PREDICTED_VARS, PARALLEL_LINES, MERIDIAN_NODES), 1.0, 6.0, ((0, 4), (2, 8))),
        "verifying_coefficients": scatter_about(key_of[1], (PREDICTED_VARS, 2, ORDERS_KEPT, DEGREE_RANGE), 0.7, 5.0, ((2, 8),), jnp.float32),
        "weighted_polynomial_values": scatter_about(key_of[2], (ORDERS_KEPT, PARALLEL_LINES, DEGREE_RANGE), PARALLEL_LINES ** -0.5, 0.75, ((0, 8),)),
        "zonal_order_values": draw_zonal_order_values(jax.random.fold_in(key_of[4], 71), 0),
    }


smooth_width = 0.1

def fourier_table(zonal_order_values, meridian_node_number):
    lon_index = jnp.arange(meridian_node_number, dtype=jnp.int32)
    phases = lon_index[:, None] * zonal_order_values[None, :] % meridian_node_number
    angles = 2.0 * math.pi / meridian_node_number * phases.astype(jnp.float32)
    zonal_order_lookup = jnp.stack([jnp.cos(angles), -jnp.sin(angles)], axis=2)
    return zonal_order_lookup.reshape(meridian_node_number, -1).astype(jnp.bfloat16)

def degree_weights(zonal_order_values, degree_count):
    degrees = jnp.arange(degree_count, dtype=jnp.int32)
    factor = jnp.where(zonal_order_values == 0, 1.0, 2.0).astype(jnp.float32)
    active = (degrees[None, :] >= zonal_order_values[:, None]).astype(jnp.float32)
    return factor[:, None] * active

def soft_abs(values):
    return jnp.sqrt(values * values + smooth_width * smooth_width) - smooth_width

def soft_sign(values):
    return values / jnp.sqrt(values * values + smooth_width * smooth_width)

def reference(predicted_grid, verifying_coefficients, weighted_polynomial_values, zonal_order_values):
    realization_pile, variable_number, parallel_line_number, meridian_node_number = predicted_grid.shape
    wave_count, _, degree_count = weighted_polynomial_values.shape
    zonal_order_lookup = fourier_table(zonal_order_values, meridian_node_number)
    divisor_factor = meridian_node_number ** (-0.5)
    sphere_coefficient_sets = (jnp.dot(predicted_grid.reshape(-1, meridian_node_number), zonal_order_lookup, preferred_element_type=jnp.float32) * divisor_factor).astype(jnp.bfloat16)
    sphere_coefficient_sets = sphere_coefficient_sets.reshape(realization_pile, variable_number, parallel_line_number, wave_count, 2).transpose(3, 0, 1, 2, 4)
    slot_target = verifying_coefficients.transpose(2, 0, 1, 3)
    highest = lax.Precision.HIGHEST

    def one_slot(pieces):
        slot_spectra, basis_rows, observed, wave_number = pieces
        coeffs = jnp.einsum('mvlr,ln->vrmn', slot_spectra.astype(jnp.float32), basis_rows.astype(jnp.float32), precision=highest)
        weights = degree_weights(wave_number[None], degree_count)[0]
        gaps = coeffs[:, :, :, None, :] - coeffs[:, :, None, :, :]
        spread_abs = lax.optimization_barrier(jnp.sum(soft_abs(gaps), axis=3))
        spread_sign = lax.optimization_barrier(jnp.sum(soft_sign(gaps), axis=3))
        misses = coeffs - observed[:, :, None, :]
        scores = lax.optimization_barrier(jnp.sum(soft_abs(misses), axis=2)) / realization_pile - lax.optimization_barrier(jnp.sum(spread_abs, axis=2)) / (2 * realization_pile * realization_pile)
        probability_error_sums = lax.optimization_barrier(jnp.sum(weights * scores, axis=2)) / degree_count
        gradients = (weights * (soft_sign(misses) / realization_pile - spread_sign / (realization_pile * realization_pile))).astype(jnp.bfloat16)
        returned = jnp.einsum('vrmn,ln->mvlr', gradients.astype(jnp.float32), basis_rows.astype(jnp.float32), precision=highest).astype(jnp.bfloat16)
        return (probability_error_sums, returned)
    probability_error_sums, returned = lax.map(one_slot, (sphere_coefficient_sets, weighted_polynomial_values, slot_target, zonal_order_values))
    coefficient_error_mean = probability_error_sums.transpose(1, 2, 0)
    returned = returned.transpose(1, 2, 3, 0, 4).reshape(-1, 2 * wave_count)
    sensitivity_grid = lax.dot_general(returned, zonal_order_lookup, (((1,), (1,)), ((), ())), preferred_element_type=jnp.float32) * divisor_factor
    prediction_sensitivity = sensitivity_grid.astype(jnp.bfloat16).reshape(predicted_grid.shape)
    return (prediction_sensitivity, coefficient_error_mean)
```

```python
import functools
import math

import jax
import jax.numpy as jnp
from jax import lax
from jax.experimental import pallas as pl
from jax.experimental.pallas import tpu as pltpu
from jax.sharding import PartitionSpec as P

smooth_width = 0.1
MESH = pl.DeviceIdType.MESH


def fourier_table(zonal_order_values, meridian_node_number):
    lon_index = jnp.arange(meridian_node_number, dtype=jnp.int32)
    quarter = meridian_node_number // 4
    phases = zonal_order_values[:, None, None] * lon_index[None, None, :]
    phases = phases + quarter * jnp.arange(2, dtype=jnp.int32)[None, :, None]
    phases = phases % meridian_node_number
    angles = 2.0 * math.pi / meridian_node_number * phases.astype(jnp.float32)
    return jnp.cos(angles).reshape(-1, meridian_node_number).astype(jnp.bfloat16)


def kernel(
    dims,
    orders_ref,
    send_ref,
    poly_ref,
    obs_hbm,
    back_ref,
    score_ref,
    obs_raw,
    obs_pad,
    poly_pad,
    recv,
    coef,
    grad,
    outgo,
    score_acc,
    obs_sem,
    send_sem,
    recv_sem,
    send_sem2,
    recv_sem2,
    score_send_sem,
    score_recv_sem,
):
    lats, enss, mem, hvars, waves, rows, degs = dims
    members = mem * enss
    q = hvars * 2 * waves
    qp = -(-q // 8) * 8
    lat = lax.axis_index("lat")
    ens = lax.axis_index("ens")
    total = lats * enss
    me = lat * enss + ens
    lanes = poly_pad.shape[1]

    def peer(i):
        t = lax.rem(me + i, total)
        return t // enss, lax.rem(t, enss)

    barrier = pltpu.get_barrier_semaphore()

    def greet(i, c):
        a, b = peer(i)
        pl.semaphore_signal(
            barrier, inc=1, device_id={"lat": a, "ens": b}, device_id_type=MESH
        )
        return c

    lax.fori_loop(1, total, greet, 0)
    obs_copy = pltpu.make_async_copy(
        obs_hbm.at[pl.ds(ens * hvars, hvars)], obs_raw, obs_sem
    )
    obs_copy.start()
    pl.semaphore_wait(barrier, total - 1)

    def send1(a, b, i):
        return pltpu.make_async_remote_copy(
            src_ref=send_ref.at[a, b],
            dst_ref=recv.at[ens, lat],
            send_sem=send_sem.at[i],
            recv_sem=recv_sem.at[ens, lat],
            device_id={"lat": a, "ens": b},
            device_id_type=MESH,
        )

    def go1(i, c):
        a, b = peer(i)
        send1(a, b, i).start()
        return c

    lax.fori_loop(1, total, go1, 0)
    recv[ens, lat] = send_ref[lat, ens]

    poly_pad[...] = jnp.zeros_like(poly_pad)
    poly_pad[:, :degs] = poly_ref[...].reshape(waves * rows, degs)
    obs_pad[...] = jnp.zeros_like(obs_pad)
    obs_copy.wait()
    for v in range(hvars):
        for r in range(2):
            for s in range(waves):
                row = (v * waves + s) * 2 + r
                obs_pad[row : row + 1, :degs] = obs_raw[v, r, s : s + 1, :]

    row_id = lax.broadcasted_iota(jnp.int32, (8, 128), 0)
    lane_id = lax.broadcasted_iota(jnp.int32, (8, 128), 1)
    row_wave = (row_id // 2) % waves
    order = jnp.full((8, 128), orders_ref[lat * waves], jnp.int32)
    for s in range(1, waves):
        order = jnp.where(row_wave == s, orders_ref[lat * waves + s], order)
    factor = jnp.where(order == 0, 1.0, 2.0).astype(jnp.float32)

    lane_wave = (lax.broadcasted_iota(jnp.int32, (rows, 128), 1) // 2) % waves
    for b in range(enss):
        for a in range(lats):

            @pl.when(jnp.logical_or(lat != a, ens != b))
            def _():
                pltpu.make_async_remote_copy(
                    src_ref=send_ref.at[a, b],
                    dst_ref=recv.at[b, a],
                    send_sem=send_sem.at[0],
                    recv_sem=recv_sem.at[b, a],
                    device_id={"lat": a, "ens": b},
                    device_id_type=MESH,
                ).wait_recv()

        chunk = recv[b].reshape(rows, 128).astype(jnp.float32)
        stacked = jnp.concatenate(
            [jnp.where(lane_wave == s, chunk, 0.0) for s in range(waves)], axis=0
        )
        lhs = stacked.T.astype(jnp.bfloat16)
        found = jnp.dot(lhs, poly_pad[...], preferred_element_type=jnp.float32)
        for k in range(mem):
            coef[b * mem + k] = found[k * qp : (k + 1) * qp]

    grad[...] = jnp.zeros_like(grad)
    eps = smooth_width * smooth_width
    inv = 1.0 / members

    def row_tile(i, c):
        r0 = pl.multiple_of(i * 8, 8)
        total_score = jnp.zeros((8, 128), jnp.float32)
        for lt in range(lanes // 128):
            ls = slice(lt * 128, (lt + 1) * 128)
            degree = lane_id + lt * 128
            w = jnp.where(
                jnp.logical_and(degree >= order, degree < degs), factor, 0.0
            )
            cs = [coef[e, pl.ds(r0, 8), ls] for e in range(members)]
            ob = obs_pad[pl.ds(r0, 8), ls]
            spread = [None] * members
            pair_sum = None
            for e in range(members):
                for f in range(e + 1, members):
                    x = cs[e] - cs[f]
                    y = x * x + eps
                    h = lax.rsqrt(y)
                    g = x * h
                    d = y * h
                    pair_sum = d if pair_sum is None else pair_sum + d
                    spread[e] = g if spread[e] is None else spread[e] + g
                    spread[f] = -g if spread[f] is None else spread[f] - g
            miss_sum = None
            for e in range(members):
                x = cs[e] - ob
                y = x * x + eps
                h = lax.rsqrt(y)
                d = y * h
                miss_sum = d if miss_sum is None else miss_sum + d
                gr = w * (x * h * inv - spread[e] * (inv * inv))
                b, k = divmod(e, mem)
                grad[b, pl.ds(pl.multiple_of(r0 + k * qp, 8), 8), ls] = gr
            pairs = members * (members - 1) // 2
            score = (miss_sum - members * smooth_width) * inv - (
                pair_sum - pairs * smooth_width
            ) * (inv * inv)
            total_score = total_score + w * score
        score_acc[pl.ds(r0, 8), :] = total_score
        return c

    score_acc[...] = jnp.zeros_like(score_acc)
    lax.fori_loop(0, qp // 8, row_tile, 0)

    for b in range(enss):
        both = lax.dot_general(
            poly_pad[...],
            grad[b].astype(jnp.bfloat16),
            (((1,), (1,)), ((), ())),
            preferred_element_type=jnp.float32,
        )
        picked = both[:rows]
        for s in range(1, waves):
            picked = jnp.where(lane_wave == s, both[s * rows : (s + 1) * rows], picked)
        outgo[b] = picked.astype(jnp.bfloat16).reshape(lats, rows // lats, 128)

    def send2(a, b, i):
        return pltpu.make_async_remote_copy(
            src_ref=outgo.at[b, a],
            dst_ref=back_ref.at[lat, ens],
            send_sem=send_sem2.at[i],
            recv_sem=recv_sem2.at[lat, ens],
            device_id={"lat": a, "ens": b},
            device_id_type=MESH,
        )

    def go2(i, c):
        a, b = peer(i)
        send2(a, b, i).start()
        return c

    lax.fori_loop(1, total, go2, 0)
    back_ref[lat, ens] = outgo[ens, lat]

    row = jnp.sum(score_acc[...].T, axis=0, keepdims=True) / degs
    score_ref[ens] = jnp.broadcast_to(row, (8, 128))

    def send3(b, i):
        return pltpu.make_async_remote_copy(
            src_ref=score_ref.at[ens],
            dst_ref=score_ref.at[ens],
            send_sem=score_send_sem.at[i],
            recv_sem=score_recv_sem.at[ens],
            device_id={"lat": lat, "ens": b},
            device_id_type=MESH,
        )

    for i in range(1, enss):
        send3(lax.rem(ens + i, enss), i).start()

    def drain(i, c):
        a, b = peer(i)
        send1(a, b, i).wait_send()
        send2(a, b, i).wait_send()
        pltpu.make_async_remote_copy(
            src_ref=outgo.at[b, a],
            dst_ref=back_ref.at[a, b],
            send_sem=send_sem2.at[0],
            recv_sem=recv_sem2.at[a, b],
            device_id={"lat": a, "ens": b},
            device_id_type=MESH,
        ).wait_recv()
        return c

    lax.fori_loop(1, total, drain, 0)
    for i in range(1, enss):
        b = lax.rem(ens + i, enss)
        send3(b, i).wait_send()
        pltpu.make_async_remote_copy(
            src_ref=score_ref.at[b],
            dst_ref=score_ref.at[b],
            send_sem=score_send_sem.at[0],
            recv_sem=score_recv_sem.at[b],
            device_id={"lat": lat, "ens": b},
            device_id_type=MESH,
        ).wait_recv()


def body(predicted_grid, verifying_coefficients, weighted_polynomial_values, zonal_order_values):
    mem, variables, block, nodes = predicted_grid.shape
    waves, rows, degs = weighted_polynomial_values.shape
    lats, enss = lax.axis_size("lat"), lax.axis_size("ens")
    hvars = variables // enss
    members = mem * enss
    q = hvars * waves * 2
    qp = -(-q // 8) * 8
    lanes = -(-degs // 128) * 128
    table = fourier_table(zonal_order_values, nodes)
    scale = nodes ** (-0.5)
    spectra = (
        lax.dot_general(
            predicted_grid.reshape(-1, nodes),
            table,
            (((1,), (1,)), ((), ())),
            preferred_element_type=jnp.float32,
        )
        * scale
    ).astype(jnp.bfloat16)
    spectra = spectra.reshape(mem, enss, hvars, block, lats, waves * 2)
    chunks = spectra.transpose(4, 1, 3, 0, 2, 5).reshape(lats, enss, block, mem, q)
    chunks = jnp.pad(chunks, ((0, 0),) * 4 + ((0, qp - q),)).reshape(
        lats, enss, block, mem * qp
    )
    chunks = jnp.pad(chunks, ((0, 0),) * 3 + ((0, 128 - mem * qp),))
    dims = (lats, enss, mem, hvars, waves, rows, degs)
    dma = pltpu.SemaphoreType.DMA
    vmem = pl.BlockSpec(memory_space=pltpu.VMEM)
    back, scores = pl.pallas_call(
        functools.partial(kernel, dims),
        out_shape=(
            jax.ShapeDtypeStruct((lats, enss, block, 128), jnp.bfloat16),
            jax.ShapeDtypeStruct((enss, 8, 128), jnp.float32),
        ),
        in_specs=[
            pl.BlockSpec(memory_space=pltpu.SMEM),
            vmem,
            vmem,
            pl.BlockSpec(memory_space=pl.ANY),
        ],
        out_specs=(vmem, vmem),
        scratch_shapes=[
            pltpu.VMEM((hvars, 2, waves, degs), jnp.float32),
            pltpu.VMEM((qp, lanes), jnp.float32),
            pltpu.VMEM((waves * rows, lanes), jnp.bfloat16),
            pltpu.VMEM((enss, lats, block, 128), jnp.bfloat16),
            pltpu.VMEM((members, qp, lanes), jnp.float32),
            pltpu.VMEM((enss, 128, lanes), jnp.float32),
            pltpu.VMEM((enss, lats, block, 128), jnp.bfloat16),
            pltpu.VMEM((128, 128), jnp.float32),
            dma(()),
            dma((lats * enss,)),
            dma((enss, lats)),
            dma((lats * enss,)),
            dma((lats, enss)),
            dma((enss,)),
            dma((enss,)),
        ],
        compiler_params=pltpu.CompilerParams(collective_id=0, has_side_effects=True),
        name="exchange",
    )(zonal_order_values, chunks, weighted_polynomial_values, verifying_coefficients)
    back = back[..., : mem * qp].reshape(lats, enss, block, mem, qp)[..., :q]
    back = back.reshape(lats, enss, block, mem, hvars, waves * 2)
    returned = back.transpose(3, 1, 4, 2, 0, 5).reshape(-1, lats * waves * 2)
    grid = (
        jnp.dot(returned, table, preferred_element_type=jnp.float32) * scale
    ).astype(jnp.bfloat16)
    scores = scores[:, 0, :q].reshape(variables, waves, 2).transpose(0, 2, 1)
    return grid.reshape(predicted_grid.shape), scores


def solution(mesh):
    placed = (P("ens", None, "lat", None), P(None, None, "lat", None), P("lat", None, None), P())
    return jax.shard_map(
        body,
        mesh=mesh,
        in_specs=placed,
        out_specs=(P("ens", None, "lat", None), P(None, None, "lat")),
        check_vma=False,
    )
```

```python
import functools
import math

import jax
import jax.numpy as jnp
from jax import lax
from jax.experimental import pallas as pl
from jax.experimental.pallas import tpu as pltpu
from jax.sharding import PartitionSpec as P

smooth_width = 0.1
MESH = pl.DeviceIdType.MESH


def kernel(
    dims,
    orders_ref,
    grid_hbm,
    poly_hbm,
    obs_hbm,
    back_out,
    table_out,
    score_out,
    grid_ref,
    poly_ref,
    table,
    select,
    spec,
    mixed,
    send_ref,
    back_ref,
    obs_raw,
    obs_pad,
    order_rows,
    poly_pad,
    recv,
    coef,
    grad,
    outgo,
    score_acc,
    score_ref,
    grid_sem,
    poly_sem,
    obs_sem,
    send_sem,
    recv_sem,
    send_sem2,
    recv_sem2,
    score_send_sem,
    score_recv_sem,
):
    lats, enss, mem, variables, hvars, waves, block, rows, degs, nodes = dims
    members = mem * enss
    parts = 2 * waves
    q = hvars * parts
    qp = -(-q // 8) * 8
    fields = mem * variables
    lat = lax.axis_index("lat")
    ens = lax.axis_index("ens")
    total = lats * enss
    me = lat * enss + ens
    lanes = poly_pad.shape[1]
    scale = nodes ** (-0.5)
    pieces = grid_sem.shape[0]
    step = fields // pieces

    def peer(i):
        t = lax.rem(me + i, total)
        return t // enss, lax.rem(t, enss)

    def grid_copy(k):
        return pltpu.make_async_copy(
            grid_hbm.at[pl.ds(k * step, step)],
            grid_ref.at[pl.ds(k * step, step)],
            grid_sem.at[k],
        )

    for k in range(pieces):
        grid_copy(k).start()
    poly_copy = pltpu.make_async_copy(poly_hbm, poly_ref, poly_sem)
    poly_copy.start()
    obs_copy = pltpu.make_async_copy(
        obs_hbm.at[pl.ds(ens * hvars, hvars)], obs_raw, obs_sem
    )
    obs_copy.start()

    barrier = pltpu.get_barrier_semaphore()

    def greet(i, c):
        a, b = peer(i)
        pl.semaphore_signal(
            barrier, inc=1, device_id={"lat": a, "ens": b}, device_id_type=MESH
        )
        return c

    lax.fori_loop(1, total, greet, 0)

    count = parts * lats
    crow = lax.broadcasted_iota(jnp.int32, (count, 128), 0)
    clane = lax.broadcasted_iota(jnp.int32, (count, 128), 1).astype(jnp.float32)
    wave_of = jnp.zeros((count, 128), jnp.float32)
    for s in range(waves):
        for a in range(lats):
            hit = crow == s * lats + a
            hit = jnp.logical_or(hit, crow == (waves + s) * lats + a)
            z = orders_ref[a * waves + s].astype(jnp.float32)
            wave_of = jnp.where(hit, z, wave_of)
    turn = jnp.where(crow >= waves * lats, nodes / 4.0, 0.0)
    for j0 in range(0, nodes, 128):
        wide = min(128, nodes - j0)
        x = wave_of * (clane + float(j0)) + turn
        x = x - float(nodes) * jnp.floor(x * (1.0 / nodes) + 0.5)
        u = 1.0 - jnp.abs(x) * (4.0 / nodes)
        half = math.pi / 2
        y = u * u
        p = jnp.full_like(u, -(half**11) / math.factorial(11))
        for n in (9, 7, 5, 3, 1):
            p = p * y + (1 - (n // 2) % 2 * 2) * half**n / math.factorial(n)
        value = (p * u).astype(jnp.bfloat16)
        table[:, j0 : j0 + wide] = value[:, :wide]

    irow = lax.broadcasted_iota(jnp.int32, (128, 128), 0)
    ilane = lax.broadcasted_iota(jnp.int32, (128, 128), 1)
    apart = ilane - irow
    eye = jnp.where(apart == 0, 1.0, 0.0).astype(jnp.bfloat16)
    for b in range(enss):
        inside = []
        for m in range(mem):
            lo = m * variables + b * hvars
            inside.append(jnp.logical_and(irow >= lo, irow < lo + hvars))
        for cc in range(parts):
            hit = None
            for m in range(mem):
                off = m * (qp - variables) + (cc - b) * hvars
                now = jnp.logical_and(inside[m], apart == off)
                hit = now if hit is None else jnp.logical_or(hit, now)
            select[cc * 128 : (cc + 1) * 128, b * 128 : (b + 1) * 128] = jnp.where(
                hit, 1.0, 0.0
            ).astype(jnp.bfloat16)

    for k in range(pieces):
        grid_copy(k).wait()
        found = lax.dot_general(
            grid_ref[k * step : (k + 1) * step].reshape(step * block, nodes),
            table[...],
            (((1,), (1,)), ((), ())),
            preferred_element_type=jnp.float32,
        )
        found = (found * scale).astype(jnp.bfloat16).astype(jnp.float32)
        for g in range(0, count, 128):
            wide = min(128, count - g)
            spec[g // 128, k * step * block : (k + 1) * step * block, :wide] = found[
                :, g : g + wide
            ]

    for t in range(block):
        line = [
            spec[g, pl.ds(t, fields, stride=block), :] for g in range(spec.shape[0])
        ]
        line = jnp.concatenate(line, axis=1)[:, :count]
        fill = jnp.zeros((128 - fields, count), jnp.float32)
        line = jnp.concatenate([line, fill], axis=0).astype(jnp.bfloat16)
        turned = lax.dot_general(
            eye[:count, :count] if count <= 128 else big_eye(count),
            line,
            (((1,), (1,)), ((), ())),
            preferred_element_type=jnp.float32,
        )
        for cc in range(parts):
            mixed[cc, pl.ds(t, lats, stride=block), :] = turned[
                cc * lats : (cc + 1) * lats
            ]
    wide_mixed = jnp.concatenate([mixed[cc] for cc in range(parts)], axis=1)
    chunks = jnp.dot(
        wide_mixed.astype(jnp.bfloat16), select[...], preferred_element_type=jnp.float32
    ).astype(jnp.bfloat16)
    for b in range(enss):
        send_ref[b] = chunks[:, b * 128 : (b + 1) * 128].reshape(lats, block, 128)

    pl.semaphore_wait(barrier, total - 1)

    def send1(a, b, i):
        return pltpu.make_async_remote_copy(
            src_ref=send_ref.at[b, a],
            dst_ref=recv.at[ens, lat],
            send_sem=send_sem.at[i],
            recv_sem=recv_sem.at[ens, lat],
            device_id={"lat": a, "ens": b},
            device_id_type=MESH,
        )

    def go1(i, c):
        a, b = peer(i)
        send1(a, b, i).start()
        return c

    lax.fori_loop(1, total, go1, 0)
    recv[ens, lat] = send_ref[ens, lat]

    table_out[...] = table[...]
    poly_pad[...] = jnp.zeros_like(poly_pad)
    poly_copy.wait()
    poly_pad[:, :degs] = poly_ref[...].reshape(waves * rows, degs)
    obs_pad[...] = jnp.zeros_like(obs_pad)
    obs_copy.wait()
    for v in range(hvars):
        for r in range(2):
            for s in range(waves):
                row = (r * waves + s) * hvars + v
                obs_pad[row : row + 1, :degs] = obs_raw[v, r, s : s + 1, :]

    def wave_at(position, s):
        hit = None
        for r in range(2):
            lo = (r * waves + s) * hvars
            now = jnp.logical_and(position >= lo, position < lo + hvars)
            hit = now if hit is None else jnp.logical_or(hit, now)
        return hit

    qrow = lax.broadcasted_iota(jnp.int32, (qp, 128), 0)
    order = jnp.full((qp, 128), orders_ref[lat * waves], jnp.int32)
    for s in range(1, waves):
        order = jnp.where(wave_at(qrow, s), orders_ref[lat * waves + s], order)
    order_rows[...] = order
    for b in range(enss):
        grad[b, mem * qp :, :] = jnp.zeros((128 - mem * qp, lanes), jnp.float32)
    score_acc[...] = jnp.zeros_like(score_acc)
    lane_id = lax.broadcasted_iota(jnp.int32, (8, 128), 1)

    where_lane = lax.broadcasted_iota(jnp.int32, (rows, 128), 1)
    lane_is = []
    for s in range(waves):
        hit = None
        for m in range(mem):
            now = wave_at(where_lane - m * qp, s)
            hit = now if hit is None else jnp.logical_or(hit, now)
        lane_is.append(hit)

    for b in range(enss):
        for a in range(lats):

            @pl.when(jnp.logical_or(lat != a, ens != b))
            def _():
                pltpu.make_async_remote_copy(
                    src_ref=send_ref.at[b, a],
                    dst_ref=recv.at[b, a],
                    send_sem=send_sem.at[0],
                    recv_sem=recv_sem.at[b, a],
                    device_id={"lat": a, "ens": b},
                    device_id_type=MESH,
                ).wait_recv()

        chunk = recv[b].reshape(rows, 128).astype(jnp.float32)
        stacked = jnp.concatenate(
            [jnp.where(lane_is[s], chunk, 0.0) for s in range(waves)], axis=0
        )
        lhs = stacked.T.astype(jnp.bfloat16)
        found = jnp.dot(lhs, poly_pad[...], preferred_element_type=jnp.float32)
        for k in range(mem):
            coef[b * mem + k] = found[k * qp : (k + 1) * qp]

    eps = smooth_width * smooth_width
    inv = 1.0 / members

    def row_tile(i, c):
        r0 = pl.multiple_of(i * 8, 8)
        total_score = jnp.zeros((8, 128), jnp.float32)
        order = order_rows[pl.ds(r0, 8), :]
        factor = jnp.where(order == 0, 1.0, 2.0).astype(jnp.float32)
        for lt in range(lanes // 128):
            ls = slice(lt * 128, (lt + 1) * 128)
            degree = lane_id + lt * 128
            w = jnp.where(
                jnp.logical_and(degree >= order, degree < degs), factor, 0.0
            )
            cs = [coef[e, pl.ds(r0, 8), ls] for e in range(members)]
            ob = obs_pad[pl.ds(r0, 8), ls]
            spread = [None] * members
            pair_sum = None
            for e in range(members):
                for f in range(e + 1, members):
                    x = cs[e] - cs[f]
                    y = x * x + eps
                    h = lax.rsqrt(y)
                    g = x * h
                    d = y * h
                    pair_sum = d if pair_sum is None else pair_sum + d
                    spread[e] = g if spread[e] is None else spread[e] + g
                    spread[f] = -g if spread[f] is None else spread[f] - g
            miss_sum = None
            for e in range(members):
                x = cs[e] - ob
                y = x * x + eps
                h = lax.rsqrt(y)
                d = y * h
                miss_sum = d if miss_sum is None else miss_sum + d
                gr = w * (x * h * inv - spread[e] * (inv * inv))
                b, k = divmod(e, mem)
                grad[b, pl.ds(pl.multiple_of(r0 + k * qp, 8), 8), ls] = gr
            pairs = members * (members - 1) // 2
            score = (miss_sum - members * smooth_width) * inv - (
                pair_sum - pairs * smooth_width
            ) * (inv * inv)
            total_score = total_score + w * score
        score_acc[pl.ds(r0, 8), :] = total_score
        return c

    lax.fori_loop(0, qp // 8, row_tile, 0)

    for b in range(enss):
        both = lax.dot_general(
            poly_pad[...],
            grad[b].astype(jnp.bfloat16),
            (((1,), (1,)), ((), ())),
            preferred_element_type=jnp.float32,
        )
        picked = both[:rows]
        for s in range(1, waves):
            picked = jnp.where(lane_is[s], both[s * rows : (s + 1) * rows], picked)
        outgo[b] = picked.astype(jnp.bfloat16).reshape(lats, block, 128)

    def send2(a, b, i):
        return pltpu.make_async_remote_copy(
            src_ref=outgo.at[b, a],
            dst_ref=back_ref.at[ens, lat],
            send_sem=send_sem2.at[i],
            recv_sem=recv_sem2.at[ens, lat],
            device_id={"lat": a, "ens": b},
            device_id_type=MESH,
        )

    def go2(i, c):
        a, b = peer(i)
        send2(a, b, i).start()
        return c

    lax.fori_loop(1, total, go2, 0)
    back_ref[ens, lat] = outgo[ens, lat]

    row = jnp.sum(score_acc[...].T, axis=0, keepdims=True) / degs
    score_ref[ens] = jnp.broadcast_to(row, (8, 128))

    def send3(b, i):
        return pltpu.make_async_remote_copy(
            src_ref=score_ref.at[ens],
            dst_ref=score_ref.at[ens],
            send_sem=score_send_sem.at[i],
            recv_sem=score_recv_sem.at[ens],
            device_id={"lat": lat, "ens": b},
            device_id_type=MESH,
        )

    for i in range(1, enss):
        send3(lax.rem(ens + i, enss), i).start()

    def drain(i, c):
        a, b = peer(i)
        send1(a, b, i).wait_send()
        pltpu.make_async_remote_copy(
            src_ref=outgo.at[b, a],
            dst_ref=back_ref.at[b, a],
            send_sem=send_sem2.at[0],
            recv_sem=recv_sem2.at[b, a],
            device_id={"lat": a, "ens": b},
            device_id_type=MESH,
        ).wait_recv()
        return c

    lax.fori_loop(1, total, drain, 0)

    merged = None
    for b in range(enss):
        part = lax.dot_general(
            back_ref[b].reshape(rows, 128),
            select[:, b * 128 : (b + 1) * 128],
            (((1,), (1,)), ((), ())),
            preferred_element_type=jnp.float32,
        )
        merged = part if merged is None else merged + part
    for cc in range(parts):
        mixed[cc] = merged[:, cc * 128 : (cc + 1) * 128]
    for t in range(block):
        line = jnp.concatenate(
            [
                mixed[cc, pl.ds(t, lats, stride=block), :] for cc in range(parts)
            ]
            + [jnp.zeros((-count % 128, 128), jnp.float32)] * (count % 128 > 0),
            axis=0,
        ).astype(jnp.bfloat16)
        turned = lax.dot_general(
            eye, line, (((1,), (1,)), ((), ())), preferred_element_type=jnp.float32
        )
        for g in range(spec.shape[0]):
            spec[g, pl.ds(t, fields, stride=block), :] = turned[
                :fields, g * 128 : (g + 1) * 128
            ]
    for g in range(0, count, 128):
        wide = min(128, count - g)
        back_out[:, g : g + wide] = spec[g // 128][:, :wide].astype(jnp.bfloat16)

    def drain2(i, c):
        a, b = peer(i)
        send2(a, b, i).wait_send()
        return c

    lax.fori_loop(1, total, drain2, 0)
    for i in range(1, enss):
        b = lax.rem(ens + i, enss)
        send3(b, i).wait_send()
        pltpu.make_async_remote_copy(
            src_ref=score_ref.at[b],
            dst_ref=score_ref.at[b],
            send_sem=score_send_sem.at[0],
            recv_sem=score_recv_sem.at[b],
            device_id={"lat": lat, "ens": b},
            device_id_type=MESH,
        ).wait_recv()
    for r in range(2):
        for s in range(waves):
            line = jnp.zeros((8, 128), jnp.float32)
            for b in range(enss):
                shift = (b - (r * waves + s)) * hvars % 128
                moved = pltpu.roll(score_ref[b], shift, 1) if shift else score_ref[b]
                mine = jnp.logical_and(
                    lane_id >= b * hvars, lane_id < (b + 1) * hvars
                )
                line = jnp.where(mine, moved, line)
            score_out[r, s : s + 1, :] = line[:1, :variables]


def big_eye(n):
    r = lax.broadcasted_iota(jnp.int32, (n, n), 0)
    c = lax.broadcasted_iota(jnp.int32, (n, n), 1)
    return jnp.where(r == c, 1.0, 0.0).astype(jnp.bfloat16)


def body(predicted_grid, verifying_coefficients, weighted_polynomial_values, zonal_order_values):
    mem, variables, block, nodes = predicted_grid.shape
    waves, rows, degs = weighted_polynomial_values.shape
    lats, enss = lax.axis_size("lat"), lax.axis_size("ens")
    hvars = variables // enss
    members = mem * enss
    parts = 2 * waves
    q = hvars * parts
    qp = -(-q // 8) * 8
    lanes = -(-degs // 128) * 128
    fields = mem * variables
    count = parts * lats
    assert mem * qp <= 128 and fields <= 128
    dims = (lats, enss, mem, variables, hvars, waves, block, rows, degs, nodes)
    dma = pltpu.SemaphoreType.DMA
    vmem = pl.BlockSpec(memory_space=pltpu.VMEM)
    hbm = pl.BlockSpec(memory_space=pl.ANY)
    f32, bf16 = jnp.float32, jnp.bfloat16
    returned, table, scores = pl.pallas_call(
        functools.partial(kernel, dims),
        out_shape=(
            jax.ShapeDtypeStruct((fields * block, count), bf16),
            jax.ShapeDtypeStruct((count, nodes), bf16),
            jax.ShapeDtypeStruct((2, waves, variables), f32),
        ),
        in_specs=[pl.BlockSpec(memory_space=pltpu.SMEM), hbm, hbm, hbm],
        out_specs=(vmem, vmem, vmem),
        scratch_shapes=[
            pltpu.VMEM((fields, block, nodes), bf16),
            pltpu.VMEM((waves, rows, degs), bf16),
            pltpu.VMEM((count, nodes), bf16),
            pltpu.VMEM((parts * 128, enss * 128), bf16),
            pltpu.VMEM((-(-count // 128), fields * block, 128), f32),
            pltpu.VMEM((parts, rows, 128), f32),
            pltpu.VMEM((enss, lats, block, 128), bf16),
            pltpu.VMEM((enss, lats, block, 128), bf16),
            pltpu.VMEM((hvars, 2, waves, degs), f32),
            pltpu.VMEM((qp, lanes), f32),
            pltpu.VMEM((qp, 128), jnp.int32),
            pltpu.VMEM((waves * rows, lanes), bf16),
            pltpu.VMEM((enss, lats, block, 128), bf16),
            pltpu.VMEM((members, qp, lanes), f32),
            pltpu.VMEM((enss, 128, lanes), f32),
            pltpu.VMEM((enss, lats, block, 128), bf16),
            pltpu.VMEM((128, 128), f32),
            pltpu.VMEM((enss, 8, 128), f32),
            dma((4,)),
            dma(()),
            dma(()),
            dma((lats * enss,)),
            dma((enss, lats)),
            dma((lats * enss,)),
            dma((enss, lats)),
            dma((enss,)),
            dma((enss,)),
        ],
        compiler_params=pltpu.CompilerParams(collective_id=0, has_side_effects=True),
        name="exchange",
    )(
        zonal_order_values,
        predicted_grid.reshape(fields, block, nodes),
        weighted_polynomial_values,
        verifying_coefficients,
    )
    grid = (
        jnp.dot(returned, table, preferred_element_type=jnp.float32)
        * nodes ** (-0.5)
    ).astype(jnp.bfloat16)
    return grid.reshape(predicted_grid.shape), scores.transpose(2, 0, 1)


def solution(mesh):
    placed = (P("ens", None, "lat", None), P(None, None, "lat", None), P("lat", None, None), P())
    return jax.shard_map(
        body,
        mesh=mesh,
        in_specs=placed,
        out_specs=(P("ens", None, "lat", None), P(None, None, "lat")),
        check_vma=False,
    )
```

```python
import functools
import math

import jax
import jax.numpy as jnp
from jax import lax
from jax.experimental import pallas as pl
from jax.experimental.pallas import tpu as pltpu
from jax.sharding import PartitionSpec as P

smooth_width = 0.1
MESH = pl.DeviceIdType.MESH


def kernel(
    dims,
    orders_hbm,
    grid_hbm,
    poly_hbm,
    obs_hbm,
    back_out,
    table_out,
    score_out,
    orders_ref,
    grid_ref,
    poly_ref,
    table,
    select,
    spec,
    mixed,
    send_ref,
    back_ref,
    obs_raw,
    obs_pad,
    order_rows,
    poly_pad,
    recv,
    coef,
    grad,
    outgo,
    score_acc,
    score_ref,
    orders_sem,
    grid_sem,
    poly_sem,
    obs_sem,
    send_sem,
    recv_sem,
    send_sem2,
    recv_sem2,
    score_send_sem,
    score_recv_sem,
):
    lats, enss, mem, variables, hvars, waves, block, rows, degs, nodes = dims
    members = mem * enss
    parts = 2 * waves
    q = hvars * parts
    qp = -(-q // 8) * 8
    fields = mem * variables
    lat = lax.axis_index("lat")
    ens = lax.axis_index("ens")
    total = lats * enss
    me = lat * enss + ens
    lanes = poly_pad.shape[1]
    scale = nodes ** (-0.5)
    pieces = grid_sem.shape[0]
    step = fields // pieces

    def peer(i):
        t = lax.rem(me + i, total)
        return t // enss, lax.rem(t, enss)

    def grid_copy(k):
        return pltpu.make_async_copy(
            grid_hbm.at[pl.ds(k * step, step)],
            grid_ref.at[pl.ds(k * step, step)],
            grid_sem.at[k],
        )

    orders_copy = pltpu.make_async_copy(orders_hbm, orders_ref, orders_sem)
    orders_copy.start()
    for k in range(pieces):
        grid_copy(k).start()
    poly_copy = pltpu.make_async_copy(poly_hbm, poly_ref, poly_sem)
    poly_copy.start()
    obs_copy = pltpu.make_async_copy(
        obs_hbm.at[pl.ds(ens * hvars, hvars)], obs_raw, obs_sem
    )
    obs_copy.start()

    def group(k):
        if enss & (enss - 1):
            return lax.rem(ens + k, enss)
        out, bit = 0, 1
        while bit < enss:
            here = lax.rem(ens // bit, 2)
            out = out + bit * (1 - here if k & bit else here)
            bit *= 2
        return out

    groups = [group(k) for k in range(enss)]

    def owners(k, f):
        def one(j, c):
            f(lax.rem(lat + j, lats), groups[k], k * lats + j)
            return c

        lax.fori_loop(0 if k else 1, lats, one, 0)

    barrier = pltpu.get_barrier_semaphore()

    def greet(i, c):
        a, b = peer(i)
        pl.semaphore_signal(
            barrier, inc=1, device_id={"lat": a, "ens": b}, device_id_type=MESH
        )
        return c

    lax.fori_loop(1, total, greet, 0)
    orders_copy.wait()

    count = parts * lats
    crow = lax.broadcasted_iota(jnp.int32, (count, 128), 0)
    clane = lax.broadcasted_iota(jnp.int32, (count, 128), 1).astype(jnp.float32)
    wave_of = jnp.zeros((count, 128), jnp.float32)
    for s in range(waves):
        for a in range(lats):
            hit = crow == s * lats + a
            hit = jnp.logical_or(hit, crow == (waves + s) * lats + a)
            z = orders_ref[a * waves + s].astype(jnp.float32)
            wave_of = jnp.where(hit, z, wave_of)
    turn = jnp.where(crow >= waves * lats, nodes / 4.0, 0.0)
    for j0 in range(0, nodes, 128):
        wide = min(128, nodes - j0)
        x = wave_of * (clane + float(j0)) + turn
        x = x - float(nodes) * jnp.floor(x * (1.0 / nodes) + 0.5)
        u = 1.0 - jnp.abs(x) * (4.0 / nodes)
        half = math.pi / 2
        y = u * u
        p = jnp.full_like(u, -(half**11) / math.factorial(11))
        for n in (9, 7, 5, 3, 1):
            p = p * y + (1 - (n // 2) % 2 * 2) * half**n / math.factorial(n)
        value = (p * u).astype(jnp.bfloat16)
        table[:, j0 : j0 + wide] = value[:, :wide]

    irow = lax.broadcasted_iota(jnp.int32, (128, 128), 0)
    ilane = lax.broadcasted_iota(jnp.int32, (128, 128), 1)
    apart = ilane - irow
    eye = jnp.where(apart == 0, 1.0, 0.0).astype(jnp.bfloat16)
    for b in range(enss):
        inside = []
        for m in range(mem):
            lo = m * variables + b * hvars
            inside.append(jnp.logical_and(irow >= lo, irow < lo + hvars))
        for cc in range(parts):
            hit = None
            for m in range(mem):
                off = m * (qp - variables) + (cc - b) * hvars
                now = jnp.logical_and(inside[m], apart == off)
                hit = now if hit is None else jnp.logical_or(hit, now)
            select[cc * 128 : (cc + 1) * 128, b * 128 : (b + 1) * 128] = jnp.where(
                hit, 1.0, 0.0
            ).astype(jnp.bfloat16)

    for k in range(pieces):
        grid_copy(k).wait()
        found = lax.dot_general(
            grid_ref[k * step : (k + 1) * step].reshape(step * block, nodes),
            table[...],
            (((1,), (1,)), ((), ())),
            preferred_element_type=jnp.float32,
        )
        found = (found * scale).astype(jnp.bfloat16).astype(jnp.float32)
        for g in range(0, count, 128):
            wide = min(128, count - g)
            spec[g // 128, k * step * block : (k + 1) * step * block, :wide] = found[
                :, g : g + wide
            ]

    for t in range(block):
        line = [
            spec[g, pl.ds(t, fields, stride=block), :] for g in range(spec.shape[0])
        ]
        line = jnp.concatenate(line, axis=1)[:, :count]
        fill = jnp.zeros((128 - fields, count), jnp.float32)
        line = jnp.concatenate([line, fill], axis=0).astype(jnp.bfloat16)
        turned = lax.dot_general(
            eye[:count, :count] if count <= 128 else big_eye(count),
            line,
            (((1,), (1,)), ((), ())),
            preferred_element_type=jnp.float32,
        )
        for cc in range(parts):
            mixed[cc, pl.ds(t, lats, stride=block), :] = turned[
                cc * lats : (cc + 1) * lats
            ]
    wide_mixed = jnp.concatenate([mixed[cc] for cc in range(parts)], axis=1)
    chunks = jnp.dot(
        wide_mixed.astype(jnp.bfloat16), select[...], preferred_element_type=jnp.float32
    ).astype(jnp.bfloat16)
    for b in range(enss):
        send_ref[b] = chunks[:, b * 128 : (b + 1) * 128].reshape(lats, block, 128)

    pl.semaphore_wait(barrier, total - 1)

    def send1(a, b, i):
        return pltpu.make_async_remote_copy(
            src_ref=send_ref.at[b, a],
            dst_ref=recv.at[ens, lat],
            send_sem=send_sem.at[i],
            recv_sem=recv_sem.at[ens, lat],
            device_id={"lat": a, "ens": b},
            device_id_type=MESH,
        )

    for k in reversed(range(enss)):
        owners(k, lambda a, b, i: send1(a, b, i).start())
    recv[ens, lat] = send_ref[ens, lat]

    table_out[...] = table[...]
    poly_pad[...] = jnp.zeros_like(poly_pad)
    poly_copy.wait()
    poly_pad[:, :degs] = poly_ref[...].reshape(waves * rows, degs)
    obs_pad[...] = jnp.zeros_like(obs_pad)
    obs_copy.wait()
    for v in range(hvars):
        for r in range(2):
            for s in range(waves):
                row = (r * waves + s) * hvars + v
                obs_pad[row : row + 1, :degs] = obs_raw[v, r, s : s + 1, :]

    def wave_at(position, s):
        hit = None
        for r in range(2):
            lo = (r * waves + s) * hvars
            now = jnp.logical_and(position >= lo, position < lo + hvars)
            hit = now if hit is None else jnp.logical_or(hit, now)
        return hit

    qrow = lax.broadcasted_iota(jnp.int32, (qp, 128), 0)
    order = jnp.full((qp, 128), orders_ref[lat * waves], jnp.int32)
    for s in range(1, waves):
        order = jnp.where(wave_at(qrow, s), orders_ref[lat * waves + s], order)
    order_rows[...] = order
    for b in range(enss):
        grad[b, mem * qp :, :] = jnp.zeros((128 - mem * qp, lanes), jnp.float32)
    score_acc[...] = jnp.zeros_like(score_acc)
    lane_id = lax.broadcasted_iota(jnp.int32, (8, 128), 1)

    where_lane = lax.broadcasted_iota(jnp.int32, (rows, 128), 1)
    lane_is = []
    for s in range(waves):
        hit = None
        for m in range(mem):
            now = wave_at(where_lane - m * qp, s)
            hit = now if hit is None else jnp.logical_or(hit, now)
        lane_is.append(hit)

    def arrive1(a, b, i):
        pltpu.make_async_remote_copy(
            src_ref=send_ref.at[b, a],
            dst_ref=recv.at[b, a],
            send_sem=send_sem.at[i],
            recv_sem=recv_sem.at[b, a],
            device_id={"lat": a, "ens": b},
            device_id_type=MESH,
        ).wait_recv()

    for g in range(enss):
        owners(g, arrive1)
        chunk = recv[groups[g]].reshape(rows, 128).astype(jnp.float32)
        stacked = jnp.concatenate(
            [jnp.where(lane_is[s], chunk, 0.0) for s in range(waves)], axis=0
        )
        lhs = stacked.T.astype(jnp.bfloat16)
        found = jnp.dot(lhs, poly_pad[...], preferred_element_type=jnp.float32)
        for k in range(mem):
            coef[g * mem + k] = found[k * qp : (k + 1) * qp]

    eps = smooth_width * smooth_width
    inv = 1.0 / members

    def row_tile(i, c):
        r0 = pl.multiple_of(i * 8, 8)
        total_score = jnp.zeros((8, 128), jnp.float32)
        order = order_rows[pl.ds(r0, 8), :]
        factor = jnp.where(order == 0, 1.0, 2.0).astype(jnp.float32)
        for lt in range(lanes // 128):
            ls = slice(lt * 128, (lt + 1) * 128)
            degree = lane_id + lt * 128
            w = jnp.where(
                jnp.logical_and(degree >= order, degree < degs), factor, 0.0
            )
            cs = [coef[e, pl.ds(r0, 8), ls] for e in range(members)]
            ob = obs_pad[pl.ds(r0, 8), ls]
            spread = [None] * members
            pair_sum = None
            for e in range(members):
                for f in range(e + 1, members):
                    x = cs[e] - cs[f]
                    y = x * x + eps
                    h = lax.rsqrt(y)
                    g = x * h
                    d = y * h
                    pair_sum = d if pair_sum is None else pair_sum + d
                    spread[e] = g if spread[e] is None else spread[e] + g
                    spread[f] = -g if spread[f] is None else spread[f] - g
            miss_sum = None
            for e in range(members):
                x = cs[e] - ob
                y = x * x + eps
                h = lax.rsqrt(y)
                d = y * h
                miss_sum = d if miss_sum is None else miss_sum + d
                gr = w * (x * h * inv - spread[e] * (inv * inv))
                b, k = divmod(e, mem)
                grad[b, pl.ds(pl.multiple_of(r0 + k * qp, 8), 8), ls] = gr
            pairs = members * (members - 1) // 2
            score = (miss_sum - members * smooth_width) * inv - (
                pair_sum - pairs * smooth_width
            ) * (inv * inv)
            total_score = total_score + w * score
        score_acc[pl.ds(r0, 8), :] = total_score
        return c

    lax.fori_loop(0, qp // 8, row_tile, 0)

    def send2(a, b, i):
        return pltpu.make_async_remote_copy(
            src_ref=outgo.at[i // lats, a],
            dst_ref=back_ref.at[ens, lat],
            send_sem=send_sem2.at[i],
            recv_sem=recv_sem2.at[ens, lat],
            device_id={"lat": a, "ens": b},
            device_id_type=MESH,
        )

    for g in reversed(range(enss)):
        both = lax.dot_general(
            poly_pad[...],
            grad[g].astype(jnp.bfloat16),
            (((1,), (1,)), ((), ())),
            preferred_element_type=jnp.float32,
        )
        picked = both[:rows]
        for s in range(1, waves):
            picked = jnp.where(lane_is[s], both[s * rows : (s + 1) * rows], picked)
        outgo[g] = picked.astype(jnp.bfloat16).reshape(lats, block, 128)
        owners(g, lambda a, b, i: send2(a, b, i).start())
    back_ref[ens, lat] = outgo[0, lat]

    row = jnp.sum(score_acc[...].T, axis=0, keepdims=True) / degs
    score_ref[ens] = jnp.broadcast_to(row, (8, 128))

    def send3(b, i):
        return pltpu.make_async_remote_copy(
            src_ref=score_ref.at[ens],
            dst_ref=score_ref.at[ens],
            send_sem=score_send_sem.at[i],
            recv_sem=score_recv_sem.at[ens],
            device_id={"lat": lat, "ens": b},
            device_id_type=MESH,
        )

    for i in range(1, enss):
        send3(lax.rem(ens + i, enss), i).start()

    def arrive2(a, b, i):
        pltpu.make_async_remote_copy(
            src_ref=outgo.at[i // lats, a],
            dst_ref=back_ref.at[b, a],
            send_sem=send_sem2.at[i],
            recv_sem=recv_sem2.at[b, a],
            device_id={"lat": a, "ens": b},
            device_id_type=MESH,
        ).wait_recv()

    for k in range(enss):
        owners(k, lambda a, b, i: send1(a, b, i).wait_send())
    merged = None
    for g in range(enss):
        owners(g, arrive2)
        b = groups[g]
        part = lax.dot_general(
            back_ref[b].reshape(rows, 128),
            select[:, pl.ds(pl.multiple_of(b * 128, 128), 128)],
            (((1,), (1,)), ((), ())),
            preferred_element_type=jnp.float32,
        )
        merged = part if merged is None else merged + part
    for cc in range(parts):
        mixed[cc] = merged[:, cc * 128 : (cc + 1) * 128]
    for t in range(block):
        line = jnp.concatenate(
            [
                mixed[cc, pl.ds(t, lats, stride=block), :] for cc in range(parts)
            ]
            + [jnp.zeros((-count % 128, 128), jnp.float32)] * (count % 128 > 0),
            axis=0,
        ).astype(jnp.bfloat16)
        turned = lax.dot_general(
            eye, line, (((1,), (1,)), ((), ())), preferred_element_type=jnp.float32
        )
        for g in range(spec.shape[0]):
            spec[g, pl.ds(t, fields, stride=block), :] = turned[
                :fields, g * 128 : (g + 1) * 128
            ]
    for g in range(0, count, 128):
        wide = min(128, count - g)
        back_out[:, g : g + wide] = spec[g // 128][:, :wide].astype(jnp.bfloat16)

    for k in range(enss):
        owners(k, lambda a, b, i: send2(a, b, i).wait_send())
    for i in range(1, enss):
        b = lax.rem(ens + i, enss)
        send3(b, i).wait_send()
        pltpu.make_async_remote_copy(
            src_ref=score_ref.at[b],
            dst_ref=score_ref.at[b],
            send_sem=score_send_sem.at[0],
            recv_sem=score_recv_sem.at[b],
            device_id={"lat": lat, "ens": b},
            device_id_type=MESH,
        ).wait_recv()
    for r in range(2):
        for s in range(waves):
            line = jnp.zeros((8, 128), jnp.float32)
            for b in range(enss):
                shift = (b - (r * waves + s)) * hvars % 128
                moved = pltpu.roll(score_ref[b], shift, 1) if shift else score_ref[b]
                mine = jnp.logical_and(
                    lane_id >= b * hvars, lane_id < (b + 1) * hvars
                )
                line = jnp.where(mine, moved, line)
            score_out[r, s : s + 1, :] = line[:1, :variables]


def finish(returned_ref, table_ref, scores_ref, grid_hbm, score_out, ready, sems):
    fields, block, nodes = ready.shape
    pieces = sems.shape[0]
    step = fields // pieces

    def copy(k):
        piece = pl.ds(k * step, step)
        return pltpu.make_async_copy(ready.at[piece], grid_hbm.at[piece], sems.at[k])

    for k in range(pieces):
        found = jnp.dot(
            returned_ref[k * step * block : (k + 1) * step * block, :],
            table_ref[...],
            preferred_element_type=jnp.float32,
        )
        found = found * nodes ** (-0.5)
        ready[k * step : (k + 1) * step] = found.reshape(step, block, nodes).astype(
            jnp.bfloat16
        )
        copy(k).start()
    score_out[...] = scores_ref[...]
    for k in range(pieces):
        copy(k).wait()


def big_eye(n):
    r = lax.broadcasted_iota(jnp.int32, (n, n), 0)
    c = lax.broadcasted_iota(jnp.int32, (n, n), 1)
    return jnp.where(r == c, 1.0, 0.0).astype(jnp.bfloat16)


def body(predicted_grid, verifying_coefficients, weighted_polynomial_values, zonal_order_values):
    mem, variables, block, nodes = predicted_grid.shape
    waves, rows, degs = weighted_polynomial_values.shape
    lats, enss = lax.axis_size("lat"), lax.axis_size("ens")
    hvars = variables // enss
    members = mem * enss
    parts = 2 * waves
    q = hvars * parts
    qp = -(-q // 8) * 8
    lanes = -(-degs // 128) * 128
    fields = mem * variables
    count = parts * lats
    assert mem * qp <= 128 and fields <= 128
    dims = (lats, enss, mem, variables, hvars, waves, block, rows, degs, nodes)
    dma = pltpu.SemaphoreType.DMA
    vmem = pl.BlockSpec(memory_space=pltpu.VMEM)
    hbm = pl.BlockSpec(memory_space=pltpu.HBM)
    f32, bf16 = jnp.float32, jnp.bfloat16
    returned, table, scores = pl.pallas_call(
        functools.partial(kernel, dims),
        out_shape=(
            jax.ShapeDtypeStruct((fields * block, count), bf16),
            jax.ShapeDtypeStruct((count, nodes), bf16),
            jax.ShapeDtypeStruct((2, waves, variables), f32),
        ),
        in_specs=[hbm] * 4,
        out_specs=(vmem, vmem, vmem),
        scratch_shapes=[
            pltpu.SMEM(zonal_order_values.shape, jnp.int32),
            pltpu.VMEM((fields, block, nodes), bf16),
            pltpu.VMEM((waves, rows, degs), bf16),
            pltpu.VMEM((count, nodes), bf16),
            pltpu.VMEM((parts * 128, enss * 128), bf16),
            pltpu.VMEM((-(-count // 128), fields * block, 128), f32),
            pltpu.VMEM((parts, rows, 128), f32),
            pltpu.VMEM((enss, lats, block, 128), bf16),
            pltpu.VMEM((enss, lats, block, 128), bf16),
            pltpu.VMEM((hvars, 2, waves, degs), f32),
            pltpu.VMEM((qp, lanes), f32),
            pltpu.VMEM((qp, 128), jnp.int32),
            pltpu.VMEM((waves * rows, lanes), bf16),
            pltpu.VMEM((enss, lats, block, 128), bf16),
            pltpu.VMEM((members, qp, lanes), f32),
            pltpu.VMEM((enss, 128, lanes), f32),
            pltpu.VMEM((enss, lats, block, 128), bf16),
            pltpu.VMEM((128, 128), f32),
            pltpu.VMEM((enss, 8, 128), f32),
            dma(()),
            dma((4,)),
            dma(()),
            dma(()),
            dma((lats * enss,)),
            dma((enss, lats)),
            dma((lats * enss,)),
            dma((enss, lats)),
            dma((enss,)),
            dma((enss,)),
        ],
        compiler_params=pltpu.CompilerParams(
            collective_id=0, has_side_effects=True, vmem_limit_bytes=32 << 20
        ),
        name="exchange",
    )(
        pltpu.with_memory_space_constraint(zonal_order_values, pltpu.HBM),
        pltpu.with_memory_space_constraint(
            predicted_grid.reshape(fields, block, nodes), pltpu.HBM
        ),
        pltpu.with_memory_space_constraint(weighted_polynomial_values, pltpu.HBM),
        pltpu.with_memory_space_constraint(verifying_coefficients, pltpu.HBM),
    )
    pieces = math.gcd(fields, 6)
    grid, scores = pl.pallas_call(
        finish,
        out_shape=(
            jax.ShapeDtypeStruct((fields, block, nodes), bf16),
            jax.ShapeDtypeStruct(scores.shape, f32),
        ),
        in_specs=[vmem, vmem, vmem],
        out_specs=(hbm, vmem),
        scratch_shapes=[pltpu.VMEM((fields, block, nodes), bf16), dma((pieces,))],
        compiler_params=pltpu.CompilerParams(vmem_limit_bytes=16 << 20),
        name="finish",
    )(returned, table, scores)
    return grid.reshape(predicted_grid.shape), scores.transpose(2, 0, 1)


def solution(mesh):
    placed = (P("ens", None, "lat", None), P(None, None, "lat", None), P("lat", None, None), P())
    return jax.shard_map(
        body,
        mesh=mesh,
        in_specs=placed,
        out_specs=(P("ens", None, "lat", None), P(None, None, "lat")),
        check_vma=False,
    )
```

```python
import functools
import math

import jax
import jax.numpy as jnp
from jax import lax
from jax.experimental import pallas as pl
from jax.experimental.pallas import tpu as pltpu
from jax.sharding import PartitionSpec as P

smooth_width = 0.1
MESH = pl.DeviceIdType.MESH


def kernel(
    dims,
    orders_hbm,
    grid_hbm,
    poly_hbm,
    obs_hbm,
    back_out,
    table_out,
    score_out,
    orders_ref,
    grid_ref,
    poly_ref,
    table,
    spread_to,
    gather_to,
    select,
    spec,
    mixed,
    send_ref,
    back_ref,
    obs_raw,
    obs_pad,
    order_rows,
    poly_pad,
    recv,
    coef,
    grad,
    outgo,
    score_acc,
    score_ref,
    orders_sem,
    grid_sem,
    poly_sem,
    obs_sem,
    send_sem,
    recv_sem,
    send_sem2,
    recv_sem2,
    score_send_sem,
    score_recv_sem,
):
    lats, enss, mem, variables, hvars, waves, block, rows, degs, nodes = dims
    members = mem * enss
    parts = 2 * waves
    q = hvars * parts
    qp = -(-q // 8) * 8
    fields = mem * variables
    lat = lax.axis_index("lat")
    ens = lax.axis_index("ens")
    total = lats * enss
    me = lat * enss + ens
    lanes = poly_pad.shape[1]
    scale = nodes ** (-0.5)
    gf = mem * hvars

    def peer(i):
        t = lax.rem(me + i, total)
        return t // enss, lax.rem(t, enss)

    def group(k):
        if enss & (enss - 1):
            return lax.rem(ens + k, enss)
        out, bit = 0, 1
        while bit < enss:
            here = lax.rem(ens // bit, 2)
            out = out + bit * (1 - here if k & bit else here)
            bit *= 2
        return out

    groups = [group(k) for k in range(enss)]

    def owners(k, f):
        def one(j, c):
            f(lax.rem(lat + j, lats), groups[k], k * lats + j)
            return c

        lax.fori_loop(0 if k else 1, lats, one, 0)

    orders_copy = pltpu.make_async_copy(orders_hbm, orders_ref, orders_sem)
    orders_copy.start()
    def grid_copy(g, m):
        return pltpu.make_async_copy(
            grid_hbm.at[pl.ds(m * variables + groups[g] * hvars, hvars)],
            grid_ref.at[g, pl.ds(m * hvars, hvars)],
            grid_sem.at[g, m],
        )

    for g in reversed(range(enss)):
        for m in range(mem):
            grid_copy(g, m).start()
    poly_copy = pltpu.make_async_copy(poly_hbm, poly_ref, poly_sem)
    poly_copy.start()
    obs_copy = pltpu.make_async_copy(
        obs_hbm.at[pl.ds(ens * hvars, hvars)], obs_raw, obs_sem
    )
    obs_copy.start()

    barrier = pltpu.get_barrier_semaphore()

    def greet(i, c):
        a, b = peer(i)
        pl.semaphore_signal(
            barrier, inc=1, device_id={"lat": a, "ens": b}, device_id_type=MESH
        )
        return c

    lax.fori_loop(1, total, greet, 0)
    orders_copy.wait()

    count = parts * lats
    crow = lax.broadcasted_iota(jnp.int32, (count, 128), 0)
    clane = lax.broadcasted_iota(jnp.int32, (count, 128), 1).astype(jnp.float32)
    wave_of = jnp.zeros((count, 128), jnp.float32)
    for s in range(waves):
        for a in range(lats):
            hit = crow == s * lats + a
            hit = jnp.logical_or(hit, crow == (waves + s) * lats + a)
            z = orders_ref[a * waves + s].astype(jnp.float32)
            wave_of = jnp.where(hit, z, wave_of)
    turn = jnp.where(crow >= waves * lats, nodes / 4.0, 0.0)
    for j0 in range(0, nodes, 128):
        wide = min(128, nodes - j0)
        x = wave_of * (clane + float(j0)) + turn
        x = x - float(nodes) * jnp.floor(x * (1.0 / nodes) + 0.5)
        u = 1.0 - jnp.abs(x) * (4.0 / nodes)
        half = math.pi / 2
        y = u * u
        p = jnp.full_like(u, -(half**11) / math.factorial(11))
        for n in (9, 7, 5, 3, 1):
            p = p * y + (1 - (n // 2) % 2 * 2) * half**n / math.factorial(n)
        value = (p * u).astype(jnp.bfloat16)
        table[:, j0 : j0 + wide] = value[:, :wide]

    irow = lax.broadcasted_iota(jnp.int32, (128, 128), 0)
    ilane = lax.broadcasted_iota(jnp.int32, (128, 128), 1)
    apart = ilane - irow
    wide_row = lax.broadcasted_iota(jnp.int32, (gf * block, 128), 0)
    wide_lane = lax.broadcasted_iota(jnp.int32, (gf * block, 128), 1)
    lag = wide_row - block * wide_lane
    for t in range(block):
        spread_to[:, t * 128 : (t + 1) * 128] = jnp.where(lag == t, 1.0, 0.0).astype(
            jnp.bfloat16
        )
    for cc in range(parts):
        hit = None
        for m in range(mem):
            now = jnp.logical_and(irow >= m * hvars, irow < (m + 1) * hvars)
            now = jnp.logical_and(now, apart == m * (qp - hvars) + cc * hvars)
            hit = now if hit is None else jnp.logical_or(hit, now)
        gather_to[cc * 128 : (cc + 1) * 128, :] = jnp.where(hit, 1.0, 0.0).astype(
            jnp.bfloat16
        )

    def prepare(g):
        for m in range(mem):
            grid_copy(g, m).wait()
        found = lax.dot_general(
            grid_ref[g].reshape(gf * block, nodes),
            table[...],
            (((1,), (1,)), ((), ())),
            preferred_element_type=jnp.float32,
        )
        found = (found * scale).T.astype(jnp.bfloat16)
        apart_t = jnp.dot(found, spread_to[...], preferred_element_type=jnp.float32)
        for t in range(block):
            for cc in range(parts):
                mixed[cc, pl.ds(t, lats, stride=block), :] = apart_t[
                    cc * lats : (cc + 1) * lats, t * 128 : (t + 1) * 128
                ]
        wide_mixed = jnp.concatenate([mixed[cc] for cc in range(parts)], axis=1)
        chunks = jnp.dot(
            wide_mixed.astype(jnp.bfloat16),
            gather_to[...],
            preferred_element_type=jnp.float32,
        )
        send_ref[groups[g]] = chunks.astype(jnp.bfloat16).reshape(lats, block, 128)

    def send1(a, b, i):
        return pltpu.make_async_remote_copy(
            src_ref=send_ref.at[b, a],
            dst_ref=recv.at[ens, lat],
            send_sem=send_sem.at[i],
            recv_sem=recv_sem.at[ens, lat],
            device_id={"lat": a, "ens": b},
            device_id_type=MESH,
        )

    waiting = []
    entered = False
    for g in reversed(range(enss)):
        prepare(g)
        waiting.append(g)
        if entered or len(waiting) >= min(2, enss):
            if not entered:
                pl.semaphore_wait(barrier, total - 1)
                entered = True
            for k in waiting:
                owners(k, lambda a, b, i: send1(a, b, i).start())
            waiting = []
    recv[ens, lat] = send_ref[ens, lat]

    eye = jnp.where(apart == 0, 1.0, 0.0).astype(jnp.bfloat16)
    for b in range(enss):
        inside = []
        for m in range(mem):
            lo = m * variables + b * hvars
            inside.append(jnp.logical_and(irow >= lo, irow < lo + hvars))
        for cc in range(parts):
            hit = None
            for m in range(mem):
                off = m * (qp - variables) + (cc - b) * hvars
                now = jnp.logical_and(inside[m], apart == off)
                hit = now if hit is None else jnp.logical_or(hit, now)
            select[cc * 128 : (cc + 1) * 128, b * 128 : (b + 1) * 128] = jnp.where(
                hit, 1.0, 0.0
            ).astype(jnp.bfloat16)

    table_out[...] = table[...]
    poly_pad[...] = jnp.zeros_like(poly_pad)
    poly_copy.wait()
    poly_pad[:, :degs] = poly_ref[...].reshape(waves * rows, degs)
    obs_pad[...] = jnp.zeros_like(obs_pad)
    obs_copy.wait()
    for v in range(hvars):
        for r in range(2):
            for s in range(waves):
                row = (r * waves + s) * hvars + v
                obs_pad[row : row + 1, :degs] = obs_raw[v, r, s : s + 1, :]

    def wave_at(position, s):
        hit = None
        for r in range(2):
            lo = (r * waves + s) * hvars
            now = jnp.logical_and(position >= lo, position < lo + hvars)
            hit = now if hit is None else jnp.logical_or(hit, now)
        return hit

    qrow = lax.broadcasted_iota(jnp.int32, (qp, 128), 0)
    order = jnp.full((qp, 128), orders_ref[lat * waves], jnp.int32)
    for s in range(1, waves):
        order = jnp.where(wave_at(qrow, s), orders_ref[lat * waves + s], order)
    order_rows[...] = order
    for b in range(enss):
        grad[b, mem * qp :, :] = jnp.zeros((128 - mem * qp, lanes), jnp.float32)
    score_acc[...] = jnp.zeros_like(score_acc)
    lane_id = lax.broadcasted_iota(jnp.int32, (8, 128), 1)

    where_lane = lax.broadcasted_iota(jnp.int32, (rows, 128), 1)
    lane_is = []
    for s in range(waves):
        hit = None
        for m in range(mem):
            now = wave_at(where_lane - m * qp, s)
            hit = now if hit is None else jnp.logical_or(hit, now)
        lane_is.append(hit)

    def arrive1(a, b, i):
        pltpu.make_async_remote_copy(
            src_ref=send_ref.at[b, a],
            dst_ref=recv.at[b, a],
            send_sem=send_sem.at[i],
            recv_sem=recv_sem.at[b, a],
            device_id={"lat": a, "ens": b},
            device_id_type=MESH,
        ).wait_recv()

    for g in range(enss):
        owners(g, arrive1)
        chunk = recv[groups[g]].reshape(rows, 128).astype(jnp.float32)
        stacked = jnp.concatenate(
            [jnp.where(lane_is[s], chunk, 0.0) for s in range(waves)], axis=0
        )
        lhs = stacked.T.astype(jnp.bfloat16)
        found = jnp.dot(lhs, poly_pad[...], preferred_element_type=jnp.float32)
        for k in range(mem):
            coef[g * mem + k] = found[k * qp : (k + 1) * qp]

    eps = smooth_width * smooth_width
    inv = 1.0 / members

    def row_tile(i, c):
        r0 = pl.multiple_of(i * 8, 8)
        total_score = jnp.zeros((8, 128), jnp.float32)
        order = order_rows[pl.ds(r0, 8), :]
        factor = jnp.where(order == 0, 1.0, 2.0).astype(jnp.float32)
        for lt in range(lanes // 128):
            ls = slice(lt * 128, (lt + 1) * 128)
            degree = lane_id + lt * 128
            w = jnp.where(
                jnp.logical_and(degree >= order, degree < degs), factor, 0.0
            )
            cs = [coef[e, pl.ds(r0, 8), ls] for e in range(members)]
            ob = obs_pad[pl.ds(r0, 8), ls]
            spread = [None] * members
            pair_sum = None
            for e in range(members):
                for f in range(e + 1, members):
                    x = cs[e] - cs[f]
                    y = x * x + eps
                    h = lax.rsqrt(y)
                    g = x * h
                    d = y * h
                    pair_sum = d if pair_sum is None else pair_sum + d
                    spread[e] = g if spread[e] is None else spread[e] + g
                    spread[f] = -g if spread[f] is None else spread[f] - g
            miss_sum = None
            for e in range(members):
                x = cs[e] - ob
                y = x * x + eps
                h = lax.rsqrt(y)
                d = y * h
                miss_sum = d if miss_sum is None else miss_sum + d
                gr = w * (x * h * inv - spread[e] * (inv * inv))
                b, k = divmod(e, mem)
                grad[b, pl.ds(pl.multiple_of(r0 + k * qp, 8), 8), ls] = gr
            pairs = members * (members - 1) // 2
            score = (miss_sum - members * smooth_width) * inv - (
                pair_sum - pairs * smooth_width
            ) * (inv * inv)
            total_score = total_score + w * score
        score_acc[pl.ds(r0, 8), :] = total_score
        return c

    lax.fori_loop(0, qp // 8, row_tile, 0)

    def send2(a, b, i):
        return pltpu.make_async_remote_copy(
            src_ref=outgo.at[i // lats, a],
            dst_ref=back_ref.at[ens, lat],
            send_sem=send_sem2.at[i],
            recv_sem=recv_sem2.at[ens, lat],
            device_id={"lat": a, "ens": b},
            device_id_type=MESH,
        )

    for g in reversed(range(enss)):
        both = lax.dot_general(
            poly_pad[...],
            grad[g].astype(jnp.bfloat16),
            (((1,), (1,)), ((), ())),
            preferred_element_type=jnp.float32,
        )
        picked = both[:rows]
        for s in range(1, waves):
            picked = jnp.where(lane_is[s], both[s * rows : (s + 1) * rows], picked)
        outgo[g] = picked.astype(jnp.bfloat16).reshape(lats, block, 128)
        owners(g, lambda a, b, i: send2(a, b, i).start())
    back_ref[ens, lat] = outgo[0, lat]

    row = jnp.sum(score_acc[...].T, axis=0, keepdims=True) / degs
    score_ref[ens] = jnp.broadcast_to(row, (8, 128))

    def send3(b, i):
        return pltpu.make_async_remote_copy(
            src_ref=score_ref.at[ens],
            dst_ref=score_ref.at[ens],
            send_sem=score_send_sem.at[i],
            recv_sem=score_recv_sem.at[ens],
            device_id={"lat": lat, "ens": b},
            device_id_type=MESH,
        )

    for i in range(1, enss):
        send3(lax.rem(ens + i, enss), i).start()

    def arrive2(a, b, i):
        pltpu.make_async_remote_copy(
            src_ref=outgo.at[i // lats, a],
            dst_ref=back_ref.at[b, a],
            send_sem=send_sem2.at[i],
            recv_sem=recv_sem2.at[b, a],
            device_id={"lat": a, "ens": b},
            device_id_type=MESH,
        ).wait_recv()

    for k in range(enss):
        owners(k, lambda a, b, i: send1(a, b, i).wait_send())
    merged = None
    for g in range(enss):
        owners(g, arrive2)
        b = groups[g]
        part = lax.dot_general(
            back_ref[b].reshape(rows, 128),
            select[:, pl.ds(pl.multiple_of(b * 128, 128), 128)],
            (((1,), (1,)), ((), ())),
            preferred_element_type=jnp.float32,
        )
        merged = part if merged is None else merged + part
    for cc in range(parts):
        mixed[cc] = merged[:, cc * 128 : (cc + 1) * 128]
    for t in range(block):
        line = jnp.concatenate(
            [
                mixed[cc, pl.ds(t, lats, stride=block), :] for cc in range(parts)
            ]
            + [jnp.zeros((-count % 128, 128), jnp.float32)] * (count % 128 > 0),
            axis=0,
        ).astype(jnp.bfloat16)
        turned = lax.dot_general(
            eye, line, (((1,), (1,)), ((), ())), preferred_element_type=jnp.float32
        )
        for g in range(spec.shape[0]):
            spec[g, pl.ds(t, fields, stride=block), :] = turned[
                :fields, g * 128 : (g + 1) * 128
            ]
    for g in range(0, count, 128):
        wide = min(128, count - g)
        back_out[:, g : g + wide] = spec[g // 128][:, :wide].astype(jnp.bfloat16)

    for k in range(enss):
        owners(k, lambda a, b, i: send2(a, b, i).wait_send())
    for i in range(1, enss):
        b = lax.rem(ens + i, enss)
        send3(b, i).wait_send()
        pltpu.make_async_remote_copy(
            src_ref=score_ref.at[b],
            dst_ref=score_ref.at[b],
            send_sem=score_send_sem.at[0],
            recv_sem=score_recv_sem.at[b],
            device_id={"lat": lat, "ens": b},
            device_id_type=MESH,
        ).wait_recv()
    for r in range(2):
        for s in range(waves):
            line = jnp.zeros((8, 128), jnp.float32)
            for b in range(enss):
                shift = (b - (r * waves + s)) * hvars % 128
                moved = pltpu.roll(score_ref[b], shift, 1) if shift else score_ref[b]
                mine = jnp.logical_and(
                    lane_id >= b * hvars, lane_id < (b + 1) * hvars
                )
                line = jnp.where(mine, moved, line)
            score_out[r, s : s + 1, :] = line[:1, :variables]


def finish(returned_ref, table_ref, scores_ref, grid_hbm, score_out, ready, sems):
    fields, block, nodes = ready.shape
    pieces = sems.shape[0]
    step = fields // pieces

    def copy(k):
        piece = pl.ds(k * step, step)
        return pltpu.make_async_copy(ready.at[piece], grid_hbm.at[piece], sems.at[k])

    for k in range(pieces):
        found = jnp.dot(
            returned_ref[k * step * block : (k + 1) * step * block, :],
            table_ref[...],
            preferred_element_type=jnp.float32,
        )
        found = found * nodes ** (-0.5)
        ready[k * step : (k + 1) * step] = found.reshape(step, block, nodes).astype(
            jnp.bfloat16
        )
        copy(k).start()
    score_out[...] = scores_ref[...]
    for k in range(pieces):
        copy(k).wait()


def body(predicted_grid, verifying_coefficients, weighted_polynomial_values, zonal_order_values):
    mem, variables, block, nodes = predicted_grid.shape
    waves, rows, degs = weighted_polynomial_values.shape
    lats, enss = lax.axis_size("lat"), lax.axis_size("ens")
    hvars = variables // enss
    members = mem * enss
    parts = 2 * waves
    q = hvars * parts
    qp = -(-q // 8) * 8
    lanes = -(-degs // 128) * 128
    fields = mem * variables
    count = parts * lats
    assert mem * qp <= 128 and fields <= 128
    dims = (lats, enss, mem, variables, hvars, waves, block, rows, degs, nodes)
    dma = pltpu.SemaphoreType.DMA
    vmem = pl.BlockSpec(memory_space=pltpu.VMEM)
    hbm = pl.BlockSpec(memory_space=pltpu.HBM)
    f32, bf16 = jnp.float32, jnp.bfloat16
    returned, table, scores = pl.pallas_call(
        functools.partial(kernel, dims),
        out_shape=(
            jax.ShapeDtypeStruct((fields * block, count), bf16),
            jax.ShapeDtypeStruct((count, nodes), bf16),
            jax.ShapeDtypeStruct((2, waves, variables), f32),
        ),
        in_specs=[hbm] * 4,
        out_specs=(vmem, vmem, vmem),
        scratch_shapes=[
            pltpu.SMEM(zonal_order_values.shape, jnp.int32),
            pltpu.VMEM((enss, mem * hvars, block, nodes), bf16),
            pltpu.VMEM((waves, rows, degs), bf16),
            pltpu.VMEM((count, nodes), bf16),
            pltpu.VMEM((mem * hvars * block, block * 128), bf16),
            pltpu.VMEM((parts * 128, 128), bf16),
            pltpu.VMEM((parts * 128, enss * 128), bf16),
            pltpu.VMEM((-(-count // 128), fields * block, 128), f32),
            pltpu.VMEM((parts, rows, 128), f32),
            pltpu.VMEM((enss, lats, block, 128), bf16),
            pltpu.VMEM((enss, lats, block, 128), bf16),
            pltpu.VMEM((hvars, 2, waves, degs), f32),
            pltpu.VMEM((qp, lanes), f32),
            pltpu.VMEM((qp, 128), jnp.int32),
            pltpu.VMEM((waves * rows, lanes), bf16),
            pltpu.VMEM((enss, lats, block, 128), bf16),
            pltpu.VMEM((members, qp, lanes), f32),
            pltpu.VMEM((enss, 128, lanes), f32),
            pltpu.VMEM((enss, lats, block, 128), bf16),
            pltpu.VMEM((128, 128), f32),
            pltpu.VMEM((enss, 8, 128), f32),
            dma(()),
            dma((enss, mem)),
            dma(()),
            dma(()),
            dma((lats * enss,)),
            dma((enss, lats)),
            dma((lats * enss,)),
            dma((enss, lats)),
            dma((enss,)),
            dma((enss,)),
        ],
        compiler_params=pltpu.CompilerParams(
            collective_id=0, has_side_effects=True, vmem_limit_bytes=32 << 20
        ),
        name="exchange",
    )(
        pltpu.with_memory_space_constraint(zonal_order_values, pltpu.HBM),
        pltpu.with_memory_space_constraint(
            predicted_grid.reshape(fields, block, nodes), pltpu.HBM
        ),
        pltpu.with_memory_space_constraint(weighted_polynomial_values, pltpu.HBM),
        pltpu.with_memory_space_constraint(verifying_coefficients, pltpu.HBM),
    )
    pieces = math.gcd(fields, 6)
    grid, scores = pl.pallas_call(
        finish,
        out_shape=(
            jax.ShapeDtypeStruct((fields, block, nodes), bf16),
            jax.ShapeDtypeStruct(scores.shape, f32),
        ),
        in_specs=[vmem, vmem, vmem],
        out_specs=(hbm, vmem),
        scratch_shapes=[pltpu.VMEM((fields, block, nodes), bf16), dma((pieces,))],
        compiler_params=pltpu.CompilerParams(vmem_limit_bytes=16 << 20),
        name="finish",
    )(returned, table, scores)
    return grid.reshape(predicted_grid.shape), scores.transpose(2, 0, 1)


def solution(mesh):
    placed = (P("ens", None, "lat", None), P(None, None, "lat", None), P("lat", None, None), P())
    return jax.shard_map(
        body,
        mesh=mesh,
        in_specs=placed,
        out_specs=(P("ens", None, "lat", None), P(None, None, "lat")),
        check_vma=False,
    )
```

```python
import functools
import math

import jax
import jax.numpy as jnp
from jax import lax
from jax.experimental import pallas as pl
from jax.experimental.pallas import tpu as pltpu
from jax.sharding import PartitionSpec as P

smooth_width = 0.1
MESH = pl.DeviceIdType.MESH


def kernel(
    dims,
    orders_hbm,
    grid_hbm,
    poly_hbm,
    obs_hbm,
    back_out,
    table_out,
    score_out,
    orders_ref,
    grid_ref,
    poly_ref,
    table,
    select,
    spec,
    mixed,
    send_ref,
    back_ref,
    obs_raw,
    obs_pad,
    order_rows,
    poly_pad,
    recv,
    coef,
    grad,
    outgo,
    score_acc,
    score_ref,
    orders_sem,
    grid_sem,
    poly_sem,
    obs_sem,
    send_sem,
    recv_sem,
    send_sem2,
    recv_sem2,
    score_send_sem,
    score_recv_sem,
):
    lats, enss, mem, variables, hvars, waves, block, rows, degs, nodes = dims
    members = mem * enss
    parts = 2 * waves
    q = hvars * parts
    qp = -(-q // 8) * 8
    fields = mem * variables
    lat = lax.axis_index("lat")
    ens = lax.axis_index("ens")
    total = lats * enss
    me = lat * enss + ens
    lanes = poly_pad.shape[1]
    scale = nodes ** (-0.5)
    pieces = grid_sem.shape[0]
    step = fields // pieces

    def peer(i):
        t = lax.rem(me + i, total)
        return t // enss, lax.rem(t, enss)

    def grid_copy(k):
        return pltpu.make_async_copy(
            grid_hbm.at[pl.ds(k * step, step)],
            grid_ref.at[pl.ds(k * step, step)],
            grid_sem.at[k],
        )

    orders_copy = pltpu.make_async_copy(orders_hbm, orders_ref, orders_sem)
    orders_copy.start()
    for k in range(pieces):
        grid_copy(k).start()
    poly_copy = pltpu.make_async_copy(poly_hbm, poly_ref, poly_sem)
    poly_copy.start()
    obs_copy = pltpu.make_async_copy(
        obs_hbm.at[pl.ds(ens * hvars, hvars)], obs_raw, obs_sem
    )
    obs_copy.start()

    def group(k):
        if enss & (enss - 1):
            return lax.rem(ens + k, enss)
        out, bit = 0, 1
        while bit < enss:
            here = lax.rem(ens // bit, 2)
            out = out + bit * (1 - here if k & bit else here)
            bit *= 2
        return out

    groups = [group(k) for k in range(enss)]

    def owners(k, f):
        def one(j, c):
            f(lax.rem(lat + j, lats), groups[k], k * lats + j)
            return c

        lax.fori_loop(0 if k else 1, lats, one, 0)

    barrier = pltpu.get_barrier_semaphore()

    def greet(i, c):
        a, b = peer(i)
        pl.semaphore_signal(
            barrier, inc=1, device_id={"lat": a, "ens": b}, device_id_type=MESH
        )
        return c

    lax.fori_loop(1, total, greet, 0)
    orders_copy.wait()

    count = parts * lats
    crow = lax.broadcasted_iota(jnp.int32, (count, 128), 0)
    clane = lax.broadcasted_iota(jnp.int32, (count, 128), 1).astype(jnp.float32)
    wave_of = jnp.zeros((count, 128), jnp.float32)
    for s in range(waves):
        for a in range(lats):
            hit = crow == s * lats + a
            hit = jnp.logical_or(hit, crow == (waves + s) * lats + a)
            z = orders_ref[a * waves + s].astype(jnp.float32)
            wave_of = jnp.where(hit, z, wave_of)
    turn = jnp.where(crow >= waves * lats, nodes / 4.0, 0.0)
    for j0 in range(0, nodes, 128):
        wide = min(128, nodes - j0)
        x = wave_of * (clane + float(j0)) + turn
        x = x - float(nodes) * jnp.floor(x * (1.0 / nodes) + 0.5)
        u = 1.0 - jnp.abs(x) * (4.0 / nodes)
        half = math.pi / 2
        y = u * u
        p = jnp.full_like(u, -(half**11) / math.factorial(11))
        for n in (9, 7, 5, 3, 1):
            p = p * y + (1 - (n // 2) % 2 * 2) * half**n / math.factorial(n)
        value = (p * u).astype(jnp.bfloat16)
        table[:, j0 : j0 + wide] = value[:, :wide]

    irow = lax.broadcasted_iota(jnp.int32, (128, 128), 0)
    ilane = lax.broadcasted_iota(jnp.int32, (128, 128), 1)
    apart = ilane - irow
    eye = jnp.where(apart == 0, 1.0, 0.0).astype(jnp.bfloat16)
    for b in range(enss):
        inside = []
        for m in range(mem):
            lo = m * variables + b * hvars
            inside.append(jnp.logical_and(irow >= lo, irow < lo + hvars))
        for cc in range(parts):
            hit = None
            for m in range(mem):
                off = m * (qp - variables) + (cc - b) * hvars
                now = jnp.logical_and(inside[m], apart == off)
                hit = now if hit is None else jnp.logical_or(hit, now)
            select[cc * 128 : (cc + 1) * 128, b * 128 : (b + 1) * 128] = jnp.where(
                hit, 1.0, 0.0
            ).astype(jnp.bfloat16)

    for k in range(pieces):
        grid_copy(k).wait()
        found = lax.dot_general(
            grid_ref[k * step : (k + 1) * step].reshape(step * block, nodes),
            table[...],
            (((1,), (1,)), ((), ())),
            preferred_element_type=jnp.float32,
        )
        found = (found * scale).astype(jnp.bfloat16).astype(jnp.float32)
        for g in range(0, count, 128):
            wide = min(128, count - g)
            spec[g // 128, k * step * block : (k + 1) * step * block, :wide] = found[
                :, g : g + wide
            ]

    for t in range(block):
        line = [
            spec[g, pl.ds(t, fields, stride=block), :] for g in range(spec.shape[0])
        ]
        line = jnp.concatenate(line, axis=1)[:, :count]
        fill = jnp.zeros((128 - fields, count), jnp.float32)
        line = jnp.concatenate([line, fill], axis=0).astype(jnp.bfloat16)
        turned = lax.dot_general(
            eye[:count, :count] if count <= 128 else big_eye(count),
            line,
            (((1,), (1,)), ((), ())),
            preferred_element_type=jnp.float32,
        )
        for cc in range(parts):
            mixed[cc, pl.ds(t, lats, stride=block), :] = turned[
                cc * lats : (cc + 1) * lats
            ]
    wide_mixed = jnp.concatenate([mixed[cc] for cc in range(parts)], axis=1)
    chunks = jnp.dot(
        wide_mixed.astype(jnp.bfloat16), select[...], preferred_element_type=jnp.float32
    ).astype(jnp.bfloat16)
    for b in range(enss):
        send_ref[b] = chunks[:, b * 128 : (b + 1) * 128].reshape(lats, block, 128)

    pl.semaphore_wait(barrier, total - 1)

    def send1(a, b, i):
        return pltpu.make_async_remote_copy(
            src_ref=send_ref.at[b, a],
            dst_ref=recv.at[ens, lat],
            send_sem=send_sem.at[i],
            recv_sem=recv_sem.at[ens, lat],
            device_id={"lat": a, "ens": b},
            device_id_type=MESH,
        )

    for k in reversed(range(enss)):
        owners(k, lambda a, b, i: send1(a, b, i).start())
    recv[ens, lat] = send_ref[ens, lat]

    table_out[...] = table[...]
    poly_pad[...] = jnp.zeros_like(poly_pad)
    poly_copy.wait()
    poly_pad[:, :degs] = poly_ref[...].reshape(waves * rows, degs)
    obs_pad[...] = jnp.zeros_like(obs_pad)
    obs_copy.wait()
    for v in range(hvars):
        for r in range(2):
            for s in range(waves):
                row = (r * waves + s) * hvars + v
                obs_pad[row : row + 1, :degs] = obs_raw[v, r, s : s + 1, :]

    def wave_at(position, s):
        hit = None
        for r in range(2):
            lo = (r * waves + s) * hvars
            now = jnp.logical_and(position >= lo, position < lo + hvars)
            hit = now if hit is None else jnp.logical_or(hit, now)
        return hit

    qrow = lax.broadcasted_iota(jnp.int32, (qp, 128), 0)
    order = jnp.full((qp, 128), orders_ref[lat * waves], jnp.int32)
    for s in range(1, waves):
        order = jnp.where(wave_at(qrow, s), orders_ref[lat * waves + s], order)
    order_rows[...] = order
    for b in range(enss):
        grad[b, mem * qp :, :] = jnp.zeros((128 - mem * qp, lanes), jnp.float32)
    score_acc[...] = jnp.zeros_like(score_acc)
    lane_id = lax.broadcasted_iota(jnp.int32, (8, 128), 1)

    where_lane = lax.broadcasted_iota(jnp.int32, (rows, 128), 1)
    lane_is = []
    for s in range(waves):
        hit = None
        for m in range(mem):
            now = wave_at(where_lane - m * qp, s)
            hit = now if hit is None else jnp.logical_or(hit, now)
        lane_is.append(hit)

    def arrive1(a, b, i):
        pltpu.make_async_remote_copy(
            src_ref=send_ref.at[b, a],
            dst_ref=recv.at[b, a],
            send_sem=send_sem.at[i],
            recv_sem=recv_sem.at[b, a],
            device_id={"lat": a, "ens": b},
            device_id_type=MESH,
        ).wait_recv()

    for g in range(enss):
        owners(g, arrive1)
        chunk = recv[groups[g]].reshape(rows, 128).astype(jnp.float32)
        stacked = jnp.concatenate(
            [jnp.where(lane_is[s], chunk, 0.0) for s in range(waves)], axis=0
        )
        lhs = stacked.T.astype(jnp.bfloat16)
        found = jnp.dot(lhs, poly_pad[...], preferred_element_type=jnp.float32)
        for k in range(mem):
            coef[g * mem + k] = found[k * qp : (k + 1) * qp]

    eps = smooth_width * smooth_width
    inv = 1.0 / members

    def row_tile(i, c):
        r0 = pl.multiple_of(i * 8, 8)
        total_score = jnp.zeros((8, 128), jnp.float32)
        order = order_rows[pl.ds(r0, 8), :]
        factor = jnp.where(order == 0, 1.0, 2.0).astype(jnp.float32)
        for lt in range(lanes // 128):
            ls = slice(lt * 128, (lt + 1) * 128)
            degree = lane_id + lt * 128
            w = jnp.where(
                jnp.logical_and(degree >= order, degree < degs), factor, 0.0
            )
            cs = [coef[e, pl.ds(r0, 8), ls] for e in range(members)]
            ob = obs_pad[pl.ds(r0, 8), ls]
            spread = [None] * members
            pair_sum = None
            for e in range(members):
                for f in range(e + 1, members):
                    x = cs[e] - cs[f]
                    y = x * x + eps
                    h = lax.rsqrt(y)
                    g = x * h
                    d = y * h
                    pair_sum = d if pair_sum is None else pair_sum + d
                    spread[e] = g if spread[e] is None else spread[e] + g
                    spread[f] = -g if spread[f] is None else spread[f] - g
            miss_sum = None
            for e in range(members):
                x = cs[e] - ob
                y = x * x + eps
                h = lax.rsqrt(y)
                d = y * h
                miss_sum = d if miss_sum is None else miss_sum + d
                gr = w * (x * h * inv - spread[e] * (inv * inv))
                b, k = divmod(e, mem)
                grad[b, pl.ds(pl.multiple_of(r0 + k * qp, 8), 8), ls] = gr
            pairs = members * (members - 1) // 2
            score = (miss_sum - members * smooth_width) * inv - (
                pair_sum - pairs * smooth_width
            ) * (inv * inv)
            total_score = total_score + w * score
        score_acc[pl.ds(r0, 8), :] = total_score
        return c

    lax.fori_loop(0, qp // 8, row_tile, 0)

    def send2(a, b, i):
        return pltpu.make_async_remote_copy(
            src_ref=outgo.at[i // lats, a],
            dst_ref=back_ref.at[ens, lat],
            send_sem=send_sem2.at[i],
            recv_sem=recv_sem2.at[ens, lat],
            device_id={"lat": a, "ens": b},
            device_id_type=MESH,
        )

    for g in reversed(range(enss)):
        both = lax.dot_general(
            poly_pad[...],
            grad[g].astype(jnp.bfloat16),
            (((1,), (1,)), ((), ())),
            preferred_element_type=jnp.float32,
        )
        picked = both[:rows]
        for s in range(1, waves):
            picked = jnp.where(lane_is[s], both[s * rows : (s + 1) * rows], picked)
        outgo[g] = picked.astype(jnp.bfloat16).reshape(lats, block, 128)
        owners(g, lambda a, b, i: send2(a, b, i).start())
    back_ref[ens, lat] = outgo[0, lat]

    row = jnp.sum(score_acc[...].T, axis=0, keepdims=True) / degs
    score_ref[ens] = jnp.broadcast_to(row, (8, 128))

    def send3(b, i):
        return pltpu.make_async_remote_copy(
            src_ref=score_ref.at[ens],
            dst_ref=score_ref.at[ens],
            send_sem=score_send_sem.at[i],
            recv_sem=score_recv_sem.at[ens],
            device_id={"lat": lat, "ens": b},
            device_id_type=MESH,
        )

    for i in range(1, enss):
        send3(lax.rem(ens + i, enss), i).start()

    def arrive2(a, b, i):
        pltpu.make_async_remote_copy(
            src_ref=outgo.at[i // lats, a],
            dst_ref=back_ref.at[b, a],
            send_sem=send_sem2.at[i],
            recv_sem=recv_sem2.at[b, a],
            device_id={"lat": a, "ens": b},
            device_id_type=MESH,
        ).wait_recv()

    for k in range(enss):
        owners(k, lambda a, b, i: send1(a, b, i).wait_send())
    merged = None
    for g in range(enss):
        owners(g, arrive2)
        b = groups[g]
        part = lax.dot_general(
            back_ref[b].reshape(rows, 128),
            select[:, pl.ds(pl.multiple_of(b * 128, 128), 128)],
            (((1,), (1,)), ((), ())),
            preferred_element_type=jnp.float32,
        )
        merged = part if merged is None else merged + part
    for cc in range(parts):
        mixed[cc] = merged[:, cc * 128 : (cc + 1) * 128]
    for t in range(block):
        line = jnp.concatenate(
            [
                mixed[cc, pl.ds(t, lats, stride=block), :] for cc in range(parts)
            ]
            + [jnp.zeros((-count % 128, 128), jnp.float32)] * (count % 128 > 0),
            axis=0,
        ).astype(jnp.bfloat16)
        turned = lax.dot_general(
            eye, line, (((1,), (1,)), ((), ())), preferred_element_type=jnp.float32
        )
        for g in range(spec.shape[0]):
            spec[g, pl.ds(t, fields, stride=block), :] = turned[
                :fields, g * 128 : (g + 1) * 128
            ]
    for g in range(0, count, 128):
        wide = min(128, count - g)
        back_out[:, g : g + wide] = spec[g // 128][:, :wide].astype(jnp.bfloat16)

    for k in range(enss):
        owners(k, lambda a, b, i: send2(a, b, i).wait_send())
    for i in range(1, enss):
        b = lax.rem(ens + i, enss)
        send3(b, i).wait_send()
        pltpu.make_async_remote_copy(
            src_ref=score_ref.at[b],
            dst_ref=score_ref.at[b],
            send_sem=score_send_sem.at[0],
            recv_sem=score_recv_sem.at[b],
            device_id={"lat": lat, "ens": b},
            device_id_type=MESH,
        ).wait_recv()
    for r in range(2):
        for s in range(waves):
            line = jnp.zeros((8, 128), jnp.float32)
            for b in range(enss):
                shift = (b - (r * waves + s)) * hvars % 128
                moved = pltpu.roll(score_ref[b], shift, 1) if shift else score_ref[b]
                mine = jnp.logical_and(
                    lane_id >= b * hvars, lane_id < (b + 1) * hvars
                )
                line = jnp.where(mine, moved, line)
            score_out[r, s : s + 1, :] = line[:1, :variables]


def finish(returned_ref, table_ref, scores_ref, grid_hbm, score_out, ready, sems):
    fields, block, nodes = ready.shape
    pieces = sems.shape[0]
    step = fields // pieces

    def copy(k):
        piece = pl.ds(k * step, step)
        return pltpu.make_async_copy(ready.at[piece], grid_hbm.at[piece], sems.at[k])

    for k in range(pieces):
        found = jnp.dot(
            returned_ref[k * step * block : (k + 1) * step * block, :],
            table_ref[...],
            preferred_element_type=jnp.float32,
        )
        found = found * nodes ** (-0.5)
        ready[k * step : (k + 1) * step] = found.reshape(step, block, nodes).astype(
            jnp.bfloat16
        )
        copy(k).start()
    score_out[...] = scores_ref[...]
    for k in range(pieces):
        copy(k).wait()


def big_eye(n):
    r = lax.broadcasted_iota(jnp.int32, (n, n), 0)
    c = lax.broadcasted_iota(jnp.int32, (n, n), 1)
    return jnp.where(r == c, 1.0, 0.0).astype(jnp.bfloat16)


def body(predicted_grid, verifying_coefficients, weighted_polynomial_values, zonal_order_values):
    mem, variables, block, nodes = predicted_grid.shape
    waves, rows, degs = weighted_polynomial_values.shape
    lats, enss = lax.axis_size("lat"), lax.axis_size("ens")
    hvars = variables // enss
    members = mem * enss
    parts = 2 * waves
    q = hvars * parts
    qp = -(-q // 8) * 8
    lanes = -(-degs // 128) * 128
    fields = mem * variables
    count = parts * lats
    assert mem * qp <= 128 and fields <= 128
    dims = (lats, enss, mem, variables, hvars, waves, block, rows, degs, nodes)
    dma = pltpu.SemaphoreType.DMA
    vmem = pl.BlockSpec(memory_space=pltpu.VMEM)
    hbm = pl.BlockSpec(memory_space=pltpu.HBM)
    f32, bf16 = jnp.float32, jnp.bfloat16
    returned, table, scores = pl.pallas_call(
        functools.partial(kernel, dims),
        out_shape=(
            jax.ShapeDtypeStruct((fields * block, count), bf16),
            jax.ShapeDtypeStruct((count, nodes), bf16),
            jax.ShapeDtypeStruct((2, waves, variables), f32),
        ),
        in_specs=[hbm] * 4,
        out_specs=(vmem, vmem, vmem),
        scratch_shapes=[
            pltpu.SMEM(zonal_order_values.shape, jnp.int32),
            pltpu.VMEM((fields, block, nodes), bf16),
            pltpu.VMEM((waves, rows, degs), bf16),
            pltpu.VMEM((count, nodes), bf16),
            pltpu.VMEM((parts * 128, enss * 128), bf16),
            pltpu.VMEM((-(-count // 128), fields * block, 128), f32),
            pltpu.VMEM((parts, rows, 128), f32),
            pltpu.VMEM((enss, lats, block, 128), bf16),
            pltpu.VMEM((enss, lats, block, 128), bf16),
            pltpu.VMEM((hvars, 2, waves, degs), f32),
            pltpu.VMEM((qp, lanes), f32),
            pltpu.VMEM((qp, 128), jnp.int32),
            pltpu.VMEM((waves * rows, lanes), bf16),
            pltpu.VMEM((enss, lats, block, 128), bf16),
            pltpu.VMEM((members, qp, lanes), f32),
            pltpu.VMEM((enss, 128, lanes), f32),
            pltpu.VMEM((enss, lats, block, 128), bf16),
            pltpu.VMEM((128, 128), f32),
            pltpu.VMEM((enss, 8, 128), f32),
            dma(()),
            dma((4,)),
            dma(()),
            dma(()),
            dma((lats * enss,)),
            dma((enss, lats)),
            dma((lats * enss,)),
            dma((enss, lats)),
            dma((enss,)),
            dma((enss,)),
        ],
        compiler_params=pltpu.CompilerParams(
            collective_id=0, has_side_effects=True, vmem_limit_bytes=32 << 20
        ),
        name="exchange",
    )(
        pltpu.with_memory_space_constraint(zonal_order_values, pltpu.HBM),
        pltpu.with_memory_space_constraint(
            predicted_grid.reshape(fields, block, nodes), pltpu.HBM
        ),
        pltpu.with_memory_space_constraint(weighted_polynomial_values, pltpu.HBM),
        pltpu.with_memory_space_constraint(verifying_coefficients, pltpu.HBM),
    )
    pieces = math.gcd(fields, 12)
    grid, scores = pl.pallas_call(
        finish,
        out_shape=(
            jax.ShapeDtypeStruct((fields, block, nodes), bf16),
            jax.ShapeDtypeStruct(scores.shape, f32),
        ),
        in_specs=[vmem, vmem, vmem],
        out_specs=(hbm, vmem),
        scratch_shapes=[pltpu.VMEM((fields, block, nodes), bf16), dma((pieces,))],
        compiler_params=pltpu.CompilerParams(vmem_limit_bytes=16 << 20),
        name="finish",
    )(returned, table, scores)
    return grid.reshape(predicted_grid.shape), scores.transpose(2, 0, 1)


def solution(mesh):
    placed = (P("ens", None, "lat", None), P(None, None, "lat", None), P("lat", None, None), P())
    return jax.shard_map(
        body,
        mesh=mesh,
        in_specs=placed,
        out_specs=(P("ens", None, "lat", None), P(None, None, "lat")),
        check_vma=False,
    )
```
